128 devices in a mesh: ctx: 32 (over z, y, core), head: 4 (over x).
Axes of the slice: x: 4, y: 4, z: 4, core: 2. Of those that a mesh axis runs over, the one named last changes fastest.
Arguments:
- queries: bfloat16 [6144, 8192], P(('ctx', 'head')), may hold values from -16 to 16
- keys: bfloat16 [6144, 1024], P(('ctx', 'head')), may hold values from -16 to 16
- values: bfloat16 [6144, 1024], P(('ctx', 'head')), may hold values from -6 to 6
- segment_ids: int32 [8, 6144], P('head', 'ctx'), may hold values from 0 to 95, as said below
- grad_out: bfloat16 [6144, 8192], P(('ctx', 'head')), may hold values from -6 to 6
Outputs:
- grad_queries: bfloat16 [6144, 8192], P('ctx', 'head')
- grad_keys: bfloat16 [6144, 1024], P('ctx', 'head')
- grad_values: bfloat16 [6144, 1024], P('ctx', 'head')
The draws below stay inside these ranges and needn't reach their ends.
Inputs may be any that keep to these rules, and one draw needn't show every extreme that they name: `segment_ids`: for each KV head and each aligned block of 192 tokens the ids start at 0 at the block's first token, never fall, and rise by at most one from token to token; for each KV head some block uses every id up to 95.
All inputs are finite; a program needn't handle non-finite values.
Results may differ from the reference program's by a relative error of at most 0.015.
Values may be sent and summed in bfloat16 or wider, within the bound.
A program may use at most 64 MiB of HBM per device.

```python
import jax
import jax.numpy as jnp
from jax import lax

QH = 64
KVH = 8
HD = 128
TOK_DEV = 192
SLOT_DEV = 96
TOKENS = 6144
SLOTS = 3072


def draw_queries(key, part):
    shape = (TOKENS, QH * HD)
    drawn = jnp.clip(jax.random.normal(jax.random.fold_in(key, 21), shape, jnp.float32), -6.0, 6.0)
    return drawn.astype(jnp.bfloat16)


def draw_keys(key, part):
    shape = (TOKENS, KVH * HD)
    drawn = jnp.clip(jax.random.normal(jax.random.fold_in(key, 31), shape, jnp.float32), -6.0, 6.0)
    return drawn.astype(jnp.bfloat16)


def draw_segment_ids(key, part):
    blocks_count = TOKENS // TOK_DEV
    heavy = jax.random.randint(jax.random.fold_in(key, 41), (KVH, 1, 1), 0, blocks_count)
    rates = jax.random.randint(jax.random.fold_in(key, 42), (KVH, blocks_count, 1), 2, 7)
    rolls = jax.random.randint(jax.random.fold_in(key, 43), (KVH, blocks_count, TOK_DEV), 0, 420)
    place = jnp.arange(TOK_DEV, dtype=jnp.int32)[None, None, :]
    starts = rolls % rates == 0
    chosen = jnp.arange(blocks_count, dtype=jnp.int32)[None, :, None] == heavy
    starts = starts | chosen & (place % 2 == 0) | (place == 0)
    segment = jnp.minimum(jnp.cumsum(starts.astype(jnp.int32), axis=2) - 1, SLOT_DEV - 1)
    return segment.reshape(KVH, TOKENS).astype(jnp.int32)


def steps_of(key, shape, shards, low, high):
    def one(position, blocks):
        heights = jax.random.uniform(jax.random.fold_in(jax.random.fold_in(key, 6), position), (blocks,), jnp.float32, low / len(shards), high / len(shards))
        return jnp.repeat(jnp.exp(heights), shape[position] // blocks).reshape((-1,) + (1,) * (len(shape) - position - 1))

    loudness = one(*shards[0])
    for cut in shards[1:]:
        loudness = loudness * one(*cut)
    return loudness


def noise(rng, extent, spread, bound, pieces=(), kind=jnp.bfloat16):
    gain = steps_of(rng, extent, pieces, -0.22, 0.18) if pieces else 1.0
    values = jax.random.normal(rng, extent, jnp.float32) * spread * gain
    return jnp.minimum(jnp.maximum(values, -bound), bound).astype(kind)


def setup_inputs(seed: int = 0) -> dict:
    arg_keys = jax.random.split(jax.random.key(seed), 6)
    return {
        "queries": draw_queries(jax.random.fold_in(arg_keys[5], 71), 0),
        "keys": draw_keys(jax.random.fold_in(arg_keys[5], 71), 0),
        "values": noise(arg_keys[2], (TOKENS, KVH * HD), 1.0, 6.0, ((0, 128),)),
        "segment_ids": draw_segment_ids(jax.random.fold_in(arg_keys[5], 71), 0),
        "grad_out": noise(arg_keys[4], (TOKENS, QH * HD), 1.0, 6.0, ((0, 128),)),
    }


masked_score = -1e30


def head_backward(operands):
    query_head, key_head, value_head, cotangent_head, segment_head = operands
    group_size = QH // KVH
    score_scale = HD ** -0.5
    blocks_count = TOKENS // TOK_DEV
    slot_picks = segment_head.reshape(blocks_count, TOK_DEV)[:, :, None] == jnp.arange(SLOT_DEV, dtype=jnp.int32)[None, None, :]
    onehot = slot_picks.astype(jnp.float32)
    counts = jnp.sum(slot_picks.astype(jnp.int32), axis=1)
    slot_sizes = jnp.maximum(counts, 1).astype(jnp.float32)[:, :, None]
    key_sums = jnp.einsum("bts,btd->bsd", onehot, key_head.reshape(blocks_count, TOK_DEV, HD).astype(jnp.float32), precision=lax.Precision.HIGHEST)
    value_sums = jnp.einsum("bts,btd->bsd", onehot, value_head.reshape(blocks_count, TOK_DEV, HD).astype(jnp.float32), precision=lax.Precision.HIGHEST)
    slot_keys = (key_sums / slot_sizes).astype(jnp.bfloat16).reshape(SLOTS, HD)
    slot_values = (value_sums / slot_sizes).astype(jnp.bfloat16).reshape(SLOTS, HD)
    live_flags = (counts > 0).reshape(SLOTS)
    slot_index = jnp.arange(SLOTS, dtype=jnp.int32)
    slot_owner = slot_index // SLOT_DEV
    slot_place = slot_index % SLOT_DEV

    def block_step(carried, inputs):
        key_grads, value_grads = carried
        block_id, query_block, key_block, value_block, cotangent_block, segment_block = inputs
        query_rows = query_block.reshape(TOK_DEV * group_size, HD)
        cotangent_rows = cotangent_block.reshape(TOK_DEV * group_size, HD)
        earlier = slot_owner[None, :] < block_id
        same = (slot_owner[None, :] == block_id) & (slot_place[None, :] < segment_block[:, None])
        visible = live_flags[None, :] & (earlier | same)
        visible = jnp.repeat(visible, group_size, axis=0)
        scores = score_scale * jnp.dot(query_rows, slot_keys.T, preferred_element_type=jnp.float32)
        own_scores = score_scale * jnp.sum(query_block.astype(jnp.float32) * key_block.astype(jnp.float32)[:, None, :], axis=2).reshape(-1)
        maxima = jnp.maximum(jnp.max(jnp.where(visible, scores, masked_score), axis=1), own_scores)
        weights = jnp.exp(jnp.where(visible, scores - maxima[:, None], masked_score))
        own_weights = jnp.exp(own_scores - maxima)
        totals = jnp.sum(weights, axis=1) + own_weights
        probabilities = weights / totals[:, None]
        own_probs = own_weights / totals
        grad_probs = jnp.dot(cotangent_rows, slot_values.T, preferred_element_type=jnp.float32)
        own_grad_probs = jnp.sum(cotangent_block.astype(jnp.float32) * value_block.astype(jnp.float32)[:, None, :], axis=2).reshape(-1)
        deltas = jnp.sum(probabilities * grad_probs, axis=1) + own_probs * own_grad_probs
        grad_scores = probabilities * (grad_probs - deltas[:, None])
        own_grad_scores = own_probs * (own_grad_probs - deltas)
        low_grads = grad_scores.astype(jnp.bfloat16)
        low_probs = probabilities.astype(jnp.bfloat16)
        key_rows = jnp.repeat(key_block.astype(jnp.float32), group_size, axis=0)
        query_grads = score_scale * (jnp.dot(low_grads, slot_keys, preferred_element_type=jnp.float32) + own_grad_scores[:, None] * key_rows)
        key_grads = key_grads + score_scale * jnp.dot(low_grads.T, query_rows, preferred_element_type=jnp.float32)
        value_grads = value_grads + jnp.dot(low_probs.T, cotangent_rows, preferred_element_type=jnp.float32)
        own_key_grads = score_scale * jnp.sum((own_grad_scores[:, None] * query_rows.astype(jnp.float32)).reshape(TOK_DEV, group_size, HD), axis=1)
        own_value_grads = jnp.sum((own_probs[:, None] * cotangent_rows.astype(jnp.float32)).reshape(TOK_DEV, group_size, HD), axis=1)
        return (key_grads, value_grads), (query_grads.astype(jnp.bfloat16).reshape(TOK_DEV, group_size * HD), own_key_grads, own_value_grads)

    zero_grads = jnp.zeros((SLOTS, HD), jnp.float32)
    inputs = (jnp.arange(blocks_count, dtype=jnp.int32),
              query_head.reshape(blocks_count, TOK_DEV, group_size, HD),
              key_head.reshape(blocks_count, TOK_DEV, HD),
              value_head.reshape(blocks_count, TOK_DEV, HD),
              cotangent_head.reshape(blocks_count, TOK_DEV, group_size, HD),
              segment_head.reshape(blocks_count, TOK_DEV))
    (key_grads, value_grads), (query_grads, own_key_grads, own_value_grads) = lax.scan(block_step, (zero_grads, zero_grads), inputs)
    token_slots = ((jnp.arange(TOKENS, dtype=jnp.int32) // TOK_DEV) * SLOT_DEV + segment_head).astype(jnp.int32)
    token_sizes = counts.reshape(SLOTS)[token_slots].astype(jnp.float32)
    grad_keys = (key_grads[token_slots] / token_sizes[:, None] + own_key_grads.reshape(TOKENS, HD)).astype(jnp.bfloat16)
    grad_values = (value_grads[token_slots] / token_sizes[:, None] + own_value_grads.reshape(TOKENS, HD)).astype(jnp.bfloat16)
    return query_grads.reshape(TOKENS, group_size * HD), grad_keys, grad_values


def reference(queries, keys, values, segment_ids, grad_out):
    group_size = QH // KVH
    query_stack = queries.reshape(TOKENS, KVH, group_size, HD).transpose(1, 0, 2, 3)
    key_stack = keys.reshape(TOKENS, KVH, HD).transpose(1, 0, 2)
    value_stack = values.reshape(TOKENS, KVH, HD).transpose(1, 0, 2)
    cotangent_stack = grad_out.reshape(TOKENS, KVH, group_size, HD).transpose(1, 0, 2, 3)
    query_grads, grad_keys, grad_values = lax.map(head_backward, (query_stack, key_stack, value_stack, cotangent_stack, segment_ids))
    return (query_grads.transpose(1, 0, 2).reshape(TOKENS, QH * HD),
            grad_keys.transpose(1, 0, 2).reshape(TOKENS, KVH * HD),
            grad_values.transpose(1, 0, 2).reshape(TOKENS, KVH * HD))
```

```python
import functools

import jax
import jax.numpy as jnp
import numpy as np
from jax import lax
from jax.experimental import pallas as pl
from jax.experimental.pallas import tpu as pltpu
from jax.sharding import PartitionSpec as P

QH = 64
KVH = 8
HD = 128
SLOT_DEV = 96
GROUP = QH // KVH
CHUNK_BLOCKS = 4
CHUNK = CHUNK_BLOCKS * SLOT_DEV
ROW_TILE = 512
HIDDEN = -1e30
DEAD_KEY = 128.0
DEAD_TEST = 64.0
SCALE = HD**-0.5
SCALE2 = SCALE * 1.4426950408889634


def dot_nt(a, b, **kw):
    return lax.dot_general(a, b, (((1,), (1,)), ((), ())), preferred_element_type=jnp.float32, **kw)


def dot_nn(a, b):
    return lax.dot_general(a, b, (((1,), (0,)), ((), ())), preferred_element_type=jnp.float32)


def attend_kernel(
    q_ref, do_ref, k_ref, v_ref, seg_ref, slots_ref,
    dq_ref, ownk_ref, ownv_ref, sg_ref,
    qa, dor, ka, kt, e_s, gp_s, mc, st, dqt, qs, dos, cols,
):
    tokens = q_ref.shape[0]
    rows = GROUP * tokens
    shards = slots_ref.shape[0] // SLOT_DEV
    total_chunks = shards // CHUNK_BLOCKS
    own = lax.axis_index("ctx")
    chunks = own // CHUNK_BLOCKS + 1
    lane = lax.broadcasted_iota(jnp.int32, (tokens, HD), 1)
    onehot = (lane == seg_ref[0]).astype(jnp.float32).astype(jnp.bfloat16)
    for h in range(GROUP):
        part = pl.ds(h * tokens, tokens)
        qa[part, 0:HD] = q_ref[:, h * HD : (h + 1) * HD]
        qa[part, HD : 2 * HD] = onehot
        dor[part, :] = do_ref[:, h * HD : (h + 1) * HD]

    kf = k_ref[...].astype(jnp.float32)
    vf = v_ref[...].astype(jnp.float32)
    ones = jnp.ones((8, HD), jnp.float32)
    for h in range(GROUP):
        part = pl.ds(h * tokens, tokens)
        qs[part, :] = q_ref[:, h * HD : (h + 1) * HD].astype(jnp.float32) * kf
        dos[part, :] = do_ref[:, h * HD : (h + 1) * HD].astype(jnp.float32) * vf
    own_s = dot_nt(ones, qs[...], precision=lax.Precision.HIGHEST)[0:1] * SCALE2
    own_g = dot_nt(ones, dos[...], precision=lax.Precision.HIGHEST)[0:1]
    st[0:1, :] = own_s
    st[1:2, :] = own_g
    st[2:3, :] = own_s
    st[3:4, :] = jnp.ones_like(own_s)
    st[4:5, :] = own_g

    srow = lax.broadcasted_iota(jnp.int32, (SLOT_DEV, HD), 0)
    slane = lax.broadcasted_iota(jnp.int32, (SLOT_DEV, HD), 1)
    diag = jnp.where(srow >= slane, HIDDEN, 0.0)

    def stat_step(c, _):
        base = pl.multiple_of(c * CHUNK, CHUNK)
        keys = slots_ref[pl.ds(base, CHUNK), 0:HD]
        ka[:, 0:HD] = keys
        for b in range(CHUNK_BLOCKS):
            block = c * CHUNK_BLOCKS + b
            part = slice(b * SLOT_DEV, (b + 1) * SLOT_DEV)
            kb = keys[part].astype(jnp.float32)
            dead = jnp.where(kb > DEAD_TEST, HIDDEN, 0.0)
            bias = jnp.where(block == own, diag, jnp.where(block > own, HIDDEN, dead))
            ka[part, HD : 2 * HD] = bias.astype(jnp.bfloat16)
        kt[c] = keys.astype(jnp.float32).T.astype(jnp.bfloat16)
        aug = ka[...]
        values = slots_ref[pl.ds(base, CHUNK), HD : 2 * HD]
        for r in range(0, rows, ROW_TILE):
            cut = slice(r, r + ROW_TILE)
            s = dot_nt(aug, qa[cut, :])
            gp = dot_nt(values, dor[cut, :])
            m_old = st[2:3, cut]
            m_new = jnp.maximum(m_old, jnp.max(s, axis=0, keepdims=True) * SCALE2)
            e = jnp.exp2(s * SCALE2 - m_new)
            back = jnp.exp2(m_old - m_new)
            e_s[c, :, cut] = e
            gp_s[c, :, cut] = gp
            mc[c, :, cut] = m_new
            st[2:3, cut] = m_new
            st[3:4, cut] = st[3:4, cut] * back + jnp.sum(e, axis=0, keepdims=True)
            st[4:5, cut] = st[4:5, cut] * back + jnp.sum(e * gp, axis=0, keepdims=True)
        return 0

    lax.fori_loop(0, chunks, stat_step, 0)

    maxima = st[2:3, :]
    inverse = 1.0 / st[3:4, :]
    deltas = st[4:5, :] * inverse
    own_p = jnp.exp2(st[0:1, :] - maxima) * inverse
    own_gs = own_p * (st[1:2, :] - deltas) * SCALE
    st[5:6, :] = deltas
    st[6:7, :] = inverse * SCALE
    inv_c = jnp.broadcast_to(inverse, (HD, rows)).T
    cols[0] = jnp.broadcast_to(own_gs, (HD, rows)).T
    cols[1] = jnp.broadcast_to(own_p, (HD, rows)).T
    qs16 = (qa[:, 0:HD].astype(jnp.float32) * (inv_c * SCALE)).astype(jnp.bfloat16)
    dos16 = (dor[...].astype(jnp.float32) * inv_c).astype(jnp.bfloat16)
    dor[...] = dos16
    dqt[...] = jnp.zeros_like(dqt)

    own_k = jnp.zeros((tokens, HD), jnp.float32)
    own_v = jnp.zeros((tokens, HD), jnp.float32)
    for h in range(GROUP):
        part = pl.ds(h * tokens, tokens)
        own_k = own_k + cols[0, part, :] * q_ref[:, h * HD : (h + 1) * HD].astype(jnp.float32)
        own_v = own_v + cols[1, part, :] * do_ref[:, h * HD : (h + 1) * HD].astype(jnp.float32)
    ownk_ref[...] = own_k
    ownv_ref[...] = own_v
    qa[:, 0:HD] = qs16

    def grad_step(c, _):
        base = pl.multiple_of(c * CHUNK, CHUNK)
        key_t = kt[c]
        acc_k = jnp.zeros((CHUNK, HD), jnp.float32)
        acc_v = jnp.zeros((CHUNK, HD), jnp.float32)
        for r in range(0, rows, ROW_TILE):
            cut = slice(r, r + ROW_TILE)
            back = jnp.exp2(mc[c, :, cut] - st[2:3, cut])
            e = e_s[c, :, cut] * back
            ds = e * (gp_s[c, :, cut] - st[5:6, cut])
            e16 = e.astype(jnp.bfloat16)
            ds16 = ds.astype(jnp.bfloat16)
            acc_v = acc_v + dot_nn(e16, dor[cut, :])
            acc_k = acc_k + dot_nn(ds16, qa[cut, 0:HD])
            dqt[:, cut] = dqt[:, cut] + dot_nn(key_t, ds16)
        sg_ref[pl.ds(base, CHUNK), 0:HD] = acc_k.astype(jnp.bfloat16)
        sg_ref[pl.ds(base, CHUNK), HD : 2 * HD] = acc_v.astype(jnp.bfloat16)
        return 0

    lax.fori_loop(0, chunks, grad_step, 0)

    def zero_step(c, _):
        base = pl.multiple_of(c * CHUNK, CHUNK)
        sg_ref[pl.ds(base, CHUNK), :] = jnp.zeros((CHUNK, 2 * HD), jnp.bfloat16)
        return 0

    lax.fori_loop(chunks, total_chunks, zero_step, 0)

    kf = k_ref[...].astype(jnp.float32)
    for h in range(GROUP):
        cut = slice(h * tokens, (h + 1) * tokens)
        part = pl.ds(h * tokens, tokens)
        qs[part, :] = cols[0, part, :] * kf
    for r in range(0, rows, ROW_TILE):
        cut = slice(r, r + ROW_TILE)
        qs[cut, :] = qs[cut, :] + (dqt[:, cut] * st[6:7, cut]).T
    for h in range(GROUP):
        part = pl.ds(h * tokens, tokens)
        dq_ref[:, h * HD : (h + 1) * HD] = qs[part, :].astype(jnp.bfloat16)


def attend(q, do, k, v, seg_cols, slots):
    tokens = q.shape[0]
    total = slots.shape[0]
    heads = k.shape[1] // HD
    rows = GROUP * tokens
    chunks = total // CHUNK
    wide = GROUP * HD
    by_head = lambda g: (0, g)
    f32, b16 = jnp.float32, jnp.bfloat16
    return pl.pallas_call(
        attend_kernel,
        grid=(heads,),
        in_specs=[
            pl.BlockSpec((tokens, wide), by_head),
            pl.BlockSpec((tokens, wide), by_head),
            pl.BlockSpec((tokens, HD), by_head),
            pl.BlockSpec((tokens, HD), by_head),
            pl.BlockSpec((1, tokens, 1), lambda g: (g, 0, 0)),
            pl.BlockSpec((total, 2 * HD), by_head),
        ],
        out_specs=[
            pl.BlockSpec((tokens, wide), by_head),
            pl.BlockSpec((tokens, HD), by_head),
            pl.BlockSpec((tokens, HD), by_head),
            pl.BlockSpec((total, 2 * HD), by_head),
        ],
        out_shape=[
            jax.ShapeDtypeStruct(q.shape, b16),
            jax.ShapeDtypeStruct(k.shape, f32),
            jax.ShapeDtypeStruct(k.shape, f32),
            jax.ShapeDtypeStruct(slots.shape, b16),
        ],
        scratch_shapes=[
            pltpu.VMEM((rows, 2 * HD), b16),
            pltpu.VMEM((rows, HD), b16),
            pltpu.VMEM((CHUNK, 2 * HD), b16),
            pltpu.VMEM((chunks, HD, CHUNK), b16),
            pltpu.VMEM((chunks, CHUNK, rows), f32),
            pltpu.VMEM((chunks, CHUNK, rows), f32),
            pltpu.VMEM((chunks, 1, rows), f32),
            pltpu.VMEM((8, rows), f32),
            pltpu.VMEM((HD, rows), f32),
            pltpu.VMEM((rows, HD), f32),
            pltpu.VMEM((rows, HD), f32),
            pltpu.VMEM((2, rows, HD), f32),
        ],
        compiler_params=pltpu.CompilerParams(vmem_limit_bytes=62 * 1024 * 1024),
        name="attend",
    )(q, do, k, v, seg_cols, slots)


def local(queries, keys, values, segment_ids, grad_out):
    swap = functools.partial(lax.all_to_all, axis_name="head", split_axis=1, concat_axis=0, tiled=True)
    keys, values = swap(keys), swap(values)
    queries, grad_out = swap(queries), swap(grad_out)
    tokens = queries.shape[0]
    kv_heads = keys.shape[1] // HD
    slot_picks = segment_ids[:, :, None] == jnp.arange(SLOT_DEV, dtype=jnp.int32)[None, None, :]
    onehot = slot_picks.astype(jnp.bfloat16)
    counts = jnp.sum(slot_picks.astype(jnp.int32), axis=1)
    slot_sizes = jnp.maximum(counts, 1).astype(jnp.float32).T[:, :, None]
    merge = lambda a: jnp.einsum(
        "gts,tgd->sgd", onehot, a.reshape(tokens, kv_heads, HD), preferred_element_type=jnp.float32
    )
    live = (counts.T > 0)[:, :, None]
    slot_rows = jnp.stack(
        [
            jnp.where(live, merge(keys) / slot_sizes, DEAD_KEY).astype(jnp.bfloat16),
            (merge(values) / slot_sizes).astype(jnp.bfloat16),
        ],
        axis=2,
    )
    slot_rows = slot_rows.reshape(SLOT_DEV, kv_heads * 2 * HD)
    gathered = lax.all_gather(slot_rows, "ctx", axis=0, tiled=True)
    grad_queries, own_k, own_v, slot_terms = attend(
        queries, grad_out, keys, values, segment_ids[:, :, None], gathered
    )
    slot_total = lax.psum_scatter(slot_terms, "ctx", scatter_dimension=0, tiled=True).astype(jnp.float32)
    slot_total = slot_total.reshape(SLOT_DEV, kv_heads, 2, HD)
    slot_spread = jnp.einsum(
        "gts,sgcd->tgcd",
        slot_picks.astype(jnp.float32),
        slot_total,
        precision=lax.Precision.HIGHEST,
    )
    token_sizes = jnp.sum(jnp.where(slot_picks, counts[:, None, :], 0), axis=2).T.astype(jnp.float32)
    spread = lambda n, own: (
        slot_spread[:, :, n] / token_sizes[..., None] + own.reshape(tokens, kv_heads, HD)
    ).astype(jnp.bfloat16).reshape(tokens, kv_heads * HD)
    return grad_queries, spread(0, own_k), spread(1, own_v)


def solution(mesh):
    both = P(("ctx", "head"), None)
    return jax.shard_map(
        local,
        mesh=mesh,
        in_specs=(both, both, both, P("head", "ctx"), both),
        out_specs=(P("ctx", "head"), P("ctx", "head"), P("ctx", "head")),
        check_vma=False,
    )
```

```python
import functools

import jax
import jax.numpy as jnp
import numpy as np
from jax import lax
from jax.experimental import pallas as pl
from jax.experimental.pallas import tpu as pltpu
from jax.sharding import PartitionSpec as P

QH = 64
KVH = 8
HD = 128
SLOT_DEV = 96
GROUP = QH // KVH
CHUNK_BLOCKS = 4
CHUNK = CHUNK_BLOCKS * SLOT_DEV
ROW_TILE = 512
HIDDEN = -1e30
DEAD_KEY = 128.0
DEAD_TEST = 64.0
MESH = pl.DeviceIdType.MESH
SCALE = HD**-0.5
SCALE2 = SCALE * 1.4426950408889634


def dot_nt(a, b, **kw):
    return lax.dot_general(a, b, (((1,), (1,)), ((), ())), preferred_element_type=jnp.float32, **kw)


def dot_nn(a, b):
    return lax.dot_general(a, b, (((1,), (0,)), ((), ())), preferred_element_type=jnp.float32)


def attend_kernel(
    q_ref, do_ref, k_ref, v_ref, seg_ref, slots_ref,
    dq_ref, ownk_ref, ownv_ref, sg_ref,
    qa, dor, ka, kt, e_s, gp_s, mc, st, dqt, qs, dos, cols,
):
    tokens = q_ref.shape[0]
    rows = GROUP * tokens
    own = lax.axis_index("ctx")
    chunks = own // CHUNK_BLOCKS + 1
    lane = lax.broadcasted_iota(jnp.int32, (tokens, HD), 1)
    onehot = (lane == seg_ref[0]).astype(jnp.float32).astype(jnp.bfloat16)
    for h in range(GROUP):
        part = pl.ds(h * tokens, tokens)
        qa[part, 0:HD] = q_ref[:, h * HD : (h + 1) * HD]
        qa[part, HD : 2 * HD] = onehot
        dor[part, :] = do_ref[:, h * HD : (h + 1) * HD]

    kf = k_ref[...].astype(jnp.float32)
    vf = v_ref[...].astype(jnp.float32)
    ones = jnp.ones((8, HD), jnp.float32)
    for h in range(GROUP):
        part = pl.ds(h * tokens, tokens)
        qs[part, :] = q_ref[:, h * HD : (h + 1) * HD].astype(jnp.float32) * kf
        dos[part, :] = do_ref[:, h * HD : (h + 1) * HD].astype(jnp.float32) * vf
    own_s = dot_nt(ones, qs[...], precision=lax.Precision.HIGHEST)[0:1] * SCALE2
    own_g = dot_nt(ones, dos[...], precision=lax.Precision.HIGHEST)[0:1]
    st[0:1, :] = own_s
    st[1:2, :] = own_g
    st[2:3, :] = own_s
    st[3:4, :] = jnp.ones_like(own_s)
    st[4:5, :] = own_g

    srow = lax.broadcasted_iota(jnp.int32, (SLOT_DEV, HD), 0)
    slane = lax.broadcasted_iota(jnp.int32, (SLOT_DEV, HD), 1)
    diag = jnp.where(srow >= slane, HIDDEN, 0.0)

    def stat_step(c, _):
        base = pl.multiple_of(c * CHUNK, CHUNK)
        keys = slots_ref[pl.ds(base, CHUNK), 0:HD]
        ka[:, 0:HD] = keys
        for b in range(CHUNK_BLOCKS):
            block = c * CHUNK_BLOCKS + b
            part = slice(b * SLOT_DEV, (b + 1) * SLOT_DEV)
            kb = keys[part].astype(jnp.float32)
            dead = jnp.where(kb > DEAD_TEST, HIDDEN, 0.0)
            bias = jnp.where(block == own, diag, jnp.where(block > own, HIDDEN, dead))
            ka[part, HD : 2 * HD] = bias.astype(jnp.bfloat16)
        kt[c] = keys.astype(jnp.float32).T.astype(jnp.bfloat16)
        aug = ka[...]
        values = slots_ref[pl.ds(base, CHUNK), HD : 2 * HD]
        for r in range(0, rows, ROW_TILE):
            cut = slice(r, r + ROW_TILE)
            s = dot_nt(aug, qa[cut, :])
            gp = dot_nt(values, dor[cut, :])
            m_old = st[2:3, cut]
            m_new = jnp.maximum(m_old, jnp.max(s, axis=0, keepdims=True) * SCALE2)
            e = jnp.exp2(s * SCALE2 - m_new)
            back = jnp.exp2(m_old - m_new)
            e_s[c, :, cut] = e
            gp_s[c, :, cut] = gp
            mc[c, :, cut] = m_new
            st[2:3, cut] = m_new
            st[3:4, cut] = st[3:4, cut] * back + jnp.sum(e, axis=0, keepdims=True)
            st[4:5, cut] = st[4:5, cut] * back + jnp.sum(e * gp, axis=0, keepdims=True)
        return 0

    lax.fori_loop(0, chunks, stat_step, 0)

    maxima = st[2:3, :]
    inverse = 1.0 / st[3:4, :]
    deltas = st[4:5, :] * inverse
    own_p = jnp.exp2(st[0:1, :] - maxima) * inverse
    own_gs = own_p * (st[1:2, :] - deltas) * SCALE
    st[5:6, :] = deltas
    st[6:7, :] = inverse * SCALE
    inv_c = jnp.broadcast_to(inverse, (HD, rows)).T
    cols[0] = jnp.broadcast_to(own_gs, (HD, rows)).T
    cols[1] = jnp.broadcast_to(own_p, (HD, rows)).T
    qs16 = (qa[:, 0:HD].astype(jnp.float32) * (inv_c * SCALE)).astype(jnp.bfloat16)
    dos16 = (dor[...].astype(jnp.float32) * inv_c).astype(jnp.bfloat16)
    dor[...] = dos16
    dqt[...] = jnp.zeros_like(dqt)

    own_k = jnp.zeros((tokens, HD), jnp.float32)
    own_v = jnp.zeros((tokens, HD), jnp.float32)
    for h in range(GROUP):
        part = pl.ds(h * tokens, tokens)
        own_k = own_k + cols[0, part, :] * q_ref[:, h * HD : (h + 1) * HD].astype(jnp.float32)
        own_v = own_v + cols[1, part, :] * do_ref[:, h * HD : (h + 1) * HD].astype(jnp.float32)
    ownk_ref[...] = own_k
    ownv_ref[...] = own_v
    qa[:, 0:HD] = qs16

    def grad_step(c, _):
        base = pl.multiple_of(c * CHUNK, CHUNK)
        key_t = kt[c]
        acc_k = jnp.zeros((CHUNK, HD), jnp.float32)
        acc_v = jnp.zeros((CHUNK, HD), jnp.float32)
        for r in range(0, rows, ROW_TILE):
            cut = slice(r, r + ROW_TILE)
            back = jnp.exp2(mc[c, :, cut] - st[2:3, cut])
            e = e_s[c, :, cut] * back
            ds = e * (gp_s[c, :, cut] - st[5:6, cut])
            e16 = e.astype(jnp.bfloat16)
            ds16 = ds.astype(jnp.bfloat16)
            acc_v = acc_v + dot_nn(e16, dor[cut, :])
            acc_k = acc_k + dot_nn(ds16, qa[cut, 0:HD])
            dqt[:, cut] = dqt[:, cut] + dot_nn(key_t, ds16)
        sg_ref[pl.ds(base, CHUNK), 0:HD] = acc_k.astype(jnp.bfloat16)
        sg_ref[pl.ds(base, CHUNK), HD : 2 * HD] = acc_v.astype(jnp.bfloat16)
        return 0

    lax.fori_loop(0, chunks, grad_step, 0)

    kf = k_ref[...].astype(jnp.float32)
    for h in range(GROUP):
        cut = slice(h * tokens, (h + 1) * tokens)
        part = pl.ds(h * tokens, tokens)
        qs[part, :] = cols[0, part, :] * kf
    for r in range(0, rows, ROW_TILE):
        cut = slice(r, r + ROW_TILE)
        qs[cut, :] = qs[cut, :] + (dqt[:, cut] * st[6:7, cut]).T
    for h in range(GROUP):
        part = pl.ds(h * tokens, tokens)
        dq_ref[:, h * HD : (h + 1) * HD] = qs[part, :].astype(jnp.bfloat16)


def attend(q, do, k, v, seg_cols, slots):
    tokens = q.shape[0]
    total = slots.shape[0]
    heads = k.shape[1] // HD
    rows = GROUP * tokens
    chunks = total // CHUNK
    wide = GROUP * HD
    by_head = lambda g: (0, g)
    f32, b16 = jnp.float32, jnp.bfloat16
    return pl.pallas_call(
        attend_kernel,
        grid=(heads,),
        in_specs=[
            pl.BlockSpec((tokens, wide), by_head),
            pl.BlockSpec((tokens, wide), by_head),
            pl.BlockSpec((tokens, HD), by_head),
            pl.BlockSpec((tokens, HD), by_head),
            pl.BlockSpec((1, tokens, 1), lambda g: (g, 0, 0)),
            pl.BlockSpec((total, 2 * HD), by_head),
        ],
        out_specs=[
            pl.BlockSpec((tokens, wide), by_head),
            pl.BlockSpec((tokens, HD), by_head),
            pl.BlockSpec((tokens, HD), by_head),
            pl.BlockSpec((total, 2 * HD), by_head),
        ],
        out_shape=[
            jax.ShapeDtypeStruct(q.shape, b16),
            jax.ShapeDtypeStruct(k.shape, f32),
            jax.ShapeDtypeStruct(k.shape, f32),
            jax.ShapeDtypeStruct(slots.shape, b16),
        ],
        scratch_shapes=[
            pltpu.VMEM((rows, 2 * HD), b16),
            pltpu.VMEM((rows, HD), b16),
            pltpu.VMEM((CHUNK, 2 * HD), b16),
            pltpu.VMEM((chunks, HD, CHUNK), b16),
            pltpu.VMEM((chunks, CHUNK, rows), f32),
            pltpu.VMEM((chunks, CHUNK, rows), f32),
            pltpu.VMEM((chunks, 1, rows), f32),
            pltpu.VMEM((8, rows), f32),
            pltpu.VMEM((HD, rows), f32),
            pltpu.VMEM((rows, HD), f32),
            pltpu.VMEM((rows, HD), f32),
            pltpu.VMEM((2, rows, HD), f32),
        ],
        compiler_params=pltpu.CompilerParams(vmem_limit_bytes=62 * 1024 * 1024),
        name="attend",
    )(q, do, k, v, seg_cols, slots)


def scatter_kernel(terms_ref, out_ref, half, sums, got, pair_send, pair_recv, send_sem, recv_sem):
    chips = terms_ref.shape[0]
    me = lax.axis_index("ctx")
    chip = me // 2
    core = me % 2
    partner = {"ctx": 2 * chip + 1 - core}
    peer = lambda k: {"ctx": 2 * k + core}

    barrier = pltpu.get_barrier_semaphore()
    pl.semaphore_signal(barrier, inc=1, device_id=partner, device_id_type=MESH)

    def greet(k, _):
        pl.semaphore_signal(barrier, inc=1, device_id=peer(k), device_id_type=MESH)
        return 0

    lax.fori_loop(chip + 1, chips, greet, 0)
    pl.semaphore_wait(barrier, chip + 1)

    def pair_copy(j):
        return pltpu.make_async_remote_copy(
            src_ref=terms_ref.at[j, 1 - core],
            dst_ref=half.at[j],
            send_sem=pair_send.at[j],
            recv_sem=pair_recv.at[j],
            device_id=partner,
            device_id_type=MESH,
        )

    def send_copy(j, source):
        return pltpu.make_async_remote_copy(
            src_ref=sums.at[j],
            dst_ref=got.at[source],
            send_sem=send_sem.at[j],
            recv_sem=recv_sem.at[source],
            device_id=peer(j),
            device_id_type=MESH,
        )

    def start_pair(j, _):
        pair_copy(j).start()
        return 0

    lax.fori_loop(0, chip + 1, start_pair, 0)

    def pass_on(j, _):
        pair_copy(j).wait_recv()
        total = terms_ref[j, core].astype(jnp.float32) + half[j].astype(jnp.float32)
        sums[j] = total.astype(jnp.bfloat16)
        send_copy(j, chip).start()
        return 0

    lax.fori_loop(0, chip, pass_on, 0)
    pair_copy(chip).wait_recv()
    out_ref[...] = terms_ref[chip, core].astype(jnp.float32) + half[chip].astype(jnp.float32)

    def take(k, _):
        send_copy(k, k).wait_recv()
        out_ref[...] = out_ref[...] + got[k].astype(jnp.float32)
        return 0

    lax.fori_loop(chip + 1, chips, take, 0)

    def end_send(j, _):
        send_copy(j, chip).wait_send()
        return 0

    lax.fori_loop(0, chip, end_send, 0)

    def end_pair(j, _):
        pair_copy(j).wait_send()
        return 0

    lax.fori_loop(0, chip + 1, end_pair, 0)


def scatter(terms):
    total, wide = terms.shape
    chips = total // (2 * SLOT_DEV)
    block = (chips, SLOT_DEV, wide)
    vmem = pl.BlockSpec(memory_space=pltpu.VMEM)
    return pl.pallas_call(
        scatter_kernel,
        in_specs=[vmem],
        out_specs=vmem,
        out_shape=jax.ShapeDtypeStruct((SLOT_DEV, wide), jnp.float32),
        scratch_shapes=[
            pltpu.VMEM(block, jnp.bfloat16),
            pltpu.VMEM(block, jnp.bfloat16),
            pltpu.VMEM(block, jnp.bfloat16),
            pltpu.SemaphoreType.DMA((chips,)),
            pltpu.SemaphoreType.DMA((chips,)),
            pltpu.SemaphoreType.DMA((chips,)),
            pltpu.SemaphoreType.DMA((chips,)),
        ],
        compiler_params=pltpu.CompilerParams(collective_id=0, has_side_effects=True),
        name="scatter",
    )(terms.reshape(chips, 2, SLOT_DEV, wide))


def local(queries, keys, values, segment_ids, grad_out):
    swap = functools.partial(lax.all_to_all, axis_name="head", split_axis=1, concat_axis=0, tiled=True)
    keys, values = swap(keys), swap(values)
    queries, grad_out = swap(queries), swap(grad_out)
    tokens = queries.shape[0]
    kv_heads = keys.shape[1] // HD
    slot_picks = segment_ids[:, :, None] == jnp.arange(SLOT_DEV, dtype=jnp.int32)[None, None, :]
    onehot = slot_picks.astype(jnp.bfloat16)
    counts = jnp.sum(slot_picks.astype(jnp.int32), axis=1)
    slot_sizes = jnp.maximum(counts, 1).astype(jnp.float32).T[:, :, None]
    merge = lambda a: jnp.einsum(
        "gts,tgd->sgd", onehot, a.reshape(tokens, kv_heads, HD), preferred_element_type=jnp.float32
    )
    live = (counts.T > 0)[:, :, None]
    slot_rows = jnp.stack(
        [
            jnp.where(live, merge(keys) / slot_sizes, DEAD_KEY).astype(jnp.bfloat16),
            (merge(values) / slot_sizes).astype(jnp.bfloat16),
        ],
        axis=2,
    )
    slot_rows = slot_rows.reshape(SLOT_DEV, kv_heads * 2 * HD)
    gathered = lax.all_gather(slot_rows, "ctx", axis=0, tiled=True)
    grad_queries, own_k, own_v, slot_terms = attend(
        queries, grad_out, keys, values, segment_ids[:, :, None], gathered
    )
    slot_total = scatter(slot_terms).reshape(SLOT_DEV, kv_heads, 2, HD)
    slot_spread = jnp.einsum(
        "gts,sgcd->tgcd",
        slot_picks.astype(jnp.float32),
        slot_total,
        precision=lax.Precision.HIGHEST,
    )
    token_sizes = jnp.sum(jnp.where(slot_picks, counts[:, None, :], 0), axis=2).T.astype(jnp.float32)
    spread = lambda n, own: (
        slot_spread[:, :, n] / token_sizes[..., None] + own.reshape(tokens, kv_heads, HD)
    ).astype(jnp.bfloat16).reshape(tokens, kv_heads * HD)
    return grad_queries, spread(0, own_k), spread(1, own_v)


def solution(mesh):
    both = P(("ctx", "head"), None)
    return jax.shard_map(
        local,
        mesh=mesh,
        in_specs=(both, both, both, P("head", "ctx"), both),
        out_specs=(P("ctx", "head"), P("ctx", "head"), P("ctx", "head")),
        check_vma=False,
    )
```

```python
import jax
import jax.numpy as jnp
import numpy as np
from jax import lax
from jax.experimental import pallas as pl
from jax.experimental.pallas import tpu as pltpu
from jax.sharding import PartitionSpec as P

QH = 64
KVH = 8
HD = 128
SLOT_DEV = 96
GROUP = QH // KVH
CHUNK_BLOCKS = 4
CHUNK = CHUNK_BLOCKS * SLOT_DEV
ROW_TILE = 512
HIDDEN = -1e30
DEAD_KEY = 128.0
DEAD_TEST = 64.0
MESH = pl.DeviceIdType.MESH
SCALE = HD**-0.5
SCALE2 = SCALE * 1.4426950408889634


def dot_nt(a, b, **kw):
    return lax.dot_general(a, b, (((1,), (1,)), ((), ())), preferred_element_type=jnp.float32, **kw)


def dot_nn(a, b):
    return lax.dot_general(a, b, (((1,), (0,)), ((), ())), preferred_element_type=jnp.float32)


def attend_kernel(
    q_ref, do_ref, k_ref, v_ref, seg_ref, slots_ref,
    dq_ref, ownk_ref, ownv_ref, sg_ref,
    qa, dor, ka, kt, e_s, gp_s, mc, st, dqt, qs, dos, cols,
):
    tokens = q_ref.shape[0]
    rows = GROUP * tokens
    own = lax.axis_index("ctx")
    chunks = own // CHUNK_BLOCKS + 1
    lane = lax.broadcasted_iota(jnp.int32, (tokens, HD), 1)
    onehot = (lane == seg_ref[0]).astype(jnp.float32).astype(jnp.bfloat16)
    for h in range(GROUP):
        part = pl.ds(h * tokens, tokens)
        qa[part, 0:HD] = q_ref[:, h * HD : (h + 1) * HD]
        qa[part, HD : 2 * HD] = onehot
        dor[part, :] = do_ref[:, h * HD : (h + 1) * HD]

    kf = k_ref[...].astype(jnp.float32)
    vf = v_ref[...].astype(jnp.float32)
    ones = jnp.ones((8, HD), jnp.float32)
    for h in range(GROUP):
        part = pl.ds(h * tokens, tokens)
        qs[part, :] = q_ref[:, h * HD : (h + 1) * HD].astype(jnp.float32) * kf
        dos[part, :] = do_ref[:, h * HD : (h + 1) * HD].astype(jnp.float32) * vf
    own_s = dot_nt(ones, qs[...], precision=lax.Precision.HIGHEST)[0:1] * SCALE2
    own_g = dot_nt(ones, dos[...], precision=lax.Precision.HIGHEST)[0:1]
    st[0:1, :] = own_s
    st[1:2, :] = own_g
    st[2:3, :] = own_s
    st[3:4, :] = jnp.ones_like(own_s)
    st[4:5, :] = own_g

    srow = lax.broadcasted_iota(jnp.int32, (SLOT_DEV, HD), 0)
    slane = lax.broadcasted_iota(jnp.int32, (SLOT_DEV, HD), 1)
    diag = jnp.where(srow >= slane, HIDDEN, 0.0)

    def stat_step(c, _):
        base = pl.multiple_of(c * CHUNK, CHUNK)
        keys = slots_ref[pl.ds(base, CHUNK), 0:HD]
        ka[:, 0:HD] = keys
        for b in range(CHUNK_BLOCKS):
            block = c * CHUNK_BLOCKS + b
            part = slice(b * SLOT_DEV, (b + 1) * SLOT_DEV)
            kb = keys[part].astype(jnp.float32)
            dead = jnp.where(kb > DEAD_TEST, HIDDEN, 0.0)
            bias = jnp.where(block == own, diag, jnp.where(block > own, HIDDEN, dead))
            ka[part, HD : 2 * HD] = bias.astype(jnp.bfloat16)
        kt[c] = keys.astype(jnp.float32).T.astype(jnp.bfloat16)
        aug = ka[...]
        values = slots_ref[pl.ds(base, CHUNK), HD : 2 * HD]
        for r in range(0, rows, ROW_TILE):
            cut = slice(r, r + ROW_TILE)
            s = dot_nt(aug, qa[cut, :])
            gp = dot_nt(values, dor[cut, :])
            m_old = st[2:3, cut]
            m_new = jnp.maximum(m_old, jnp.max(s, axis=0, keepdims=True) * SCALE2)
            e = jnp.exp2(s * SCALE2 - m_new)
            back = jnp.exp2(m_old - m_new)
            e_s[c, :, cut] = e
            gp_s[c, :, cut] = gp
            mc[c, :, cut] = m_new
            st[2:3, cut] = m_new
            st[3:4, cut] = st[3:4, cut] * back + jnp.sum(e, axis=0, keepdims=True)
            st[4:5, cut] = st[4:5, cut] * back + jnp.sum(e * gp, axis=0, keepdims=True)
        return 0

    lax.fori_loop(0, chunks, stat_step, 0)

    maxima = st[2:3, :]
    inverse = 1.0 / st[3:4, :]
    deltas = st[4:5, :] * inverse
    own_p = jnp.exp2(st[0:1, :] - maxima) * inverse
    own_gs = own_p * (st[1:2, :] - deltas) * SCALE
    st[5:6, :] = deltas
    st[6:7, :] = inverse * SCALE
    inv_c = jnp.broadcast_to(inverse, (HD, rows)).T
    cols[0] = jnp.broadcast_to(own_gs, (HD, rows)).T
    cols[1] = jnp.broadcast_to(own_p, (HD, rows)).T
    qs16 = (qa[:, 0:HD].astype(jnp.float32) * (inv_c * SCALE)).astype(jnp.bfloat16)
    dos16 = (dor[...].astype(jnp.float32) * inv_c).astype(jnp.bfloat16)
    dor[...] = dos16
    dqt[...] = jnp.zeros_like(dqt)

    own_k = jnp.zeros((tokens, HD), jnp.float32)
    own_v = jnp.zeros((tokens, HD), jnp.float32)
    for h in range(GROUP):
        part = pl.ds(h * tokens, tokens)
        own_k = own_k + cols[0, part, :] * q_ref[:, h * HD : (h + 1) * HD].astype(jnp.float32)
        own_v = own_v + cols[1, part, :] * do_ref[:, h * HD : (h + 1) * HD].astype(jnp.float32)
    ownk_ref[...] = own_k
    ownv_ref[...] = own_v
    qa[:, 0:HD] = qs16

    def grad_step(c, _):
        base = pl.multiple_of(c * CHUNK, CHUNK)
        key_t = kt[c]
        acc_k = jnp.zeros((CHUNK, HD), jnp.float32)
        acc_v = jnp.zeros((CHUNK, HD), jnp.float32)
        for r in range(0, rows, ROW_TILE):
            cut = slice(r, r + ROW_TILE)
            back = jnp.exp2(mc[c, :, cut] - st[2:3, cut])
            e = e_s[c, :, cut] * back
            ds = e * (gp_s[c, :, cut] - st[5:6, cut])
            e16 = e.astype(jnp.bfloat16)
            ds16 = ds.astype(jnp.bfloat16)
            acc_v = acc_v + dot_nn(e16, dor[cut, :])
            acc_k = acc_k + dot_nn(ds16, qa[cut, 0:HD])
            dqt[:, cut] = dqt[:, cut] + dot_nn(key_t, ds16)
        sg_ref[pl.ds(base, CHUNK), 0:HD] = acc_k.astype(jnp.bfloat16)
        sg_ref[pl.ds(base, CHUNK), HD : 2 * HD] = acc_v.astype(jnp.bfloat16)
        return 0

    lax.fori_loop(0, chunks, grad_step, 0)

    kf = k_ref[...].astype(jnp.float32)
    for h in range(GROUP):
        cut = slice(h * tokens, (h + 1) * tokens)
        part = pl.ds(h * tokens, tokens)
        qs[part, :] = cols[0, part, :] * kf
    for r in range(0, rows, ROW_TILE):
        cut = slice(r, r + ROW_TILE)
        qs[cut, :] = qs[cut, :] + (dqt[:, cut] * st[6:7, cut]).T
    for h in range(GROUP):
        part = pl.ds(h * tokens, tokens)
        dq_ref[:, h * HD : (h + 1) * HD] = qs[part, :].astype(jnp.bfloat16)


def attend(q, do, k, v, seg_cols, slots):
    tokens = q.shape[0]
    total = slots.shape[0]
    heads = k.shape[1] // HD
    rows = GROUP * tokens
    chunks = total // CHUNK
    wide = GROUP * HD
    by_head = lambda g: (0, g)
    f32, b16 = jnp.float32, jnp.bfloat16
    return pl.pallas_call(
        attend_kernel,
        grid=(heads,),
        in_specs=[
            pl.BlockSpec((tokens, wide), by_head),
            pl.BlockSpec((tokens, wide), by_head),
            pl.BlockSpec((tokens, HD), by_head),
            pl.BlockSpec((tokens, HD), by_head),
            pl.BlockSpec((1, tokens, 1), lambda g: (g, 0, 0)),
            pl.BlockSpec((total, 2 * HD), by_head),
        ],
        out_specs=[
            pl.BlockSpec((tokens, wide), by_head),
            pl.BlockSpec((tokens, HD), by_head),
            pl.BlockSpec((tokens, HD), by_head),
            pl.BlockSpec((total, 2 * HD), by_head),
        ],
        out_shape=[
            jax.ShapeDtypeStruct(q.shape, b16),
            jax.ShapeDtypeStruct(k.shape, f32),
            jax.ShapeDtypeStruct(k.shape, f32),
            jax.ShapeDtypeStruct(slots.shape, b16),
        ],
        scratch_shapes=[
            pltpu.VMEM((rows, 2 * HD), b16),
            pltpu.VMEM((rows, HD), b16),
            pltpu.VMEM((CHUNK, 2 * HD), b16),
            pltpu.VMEM((chunks, HD, CHUNK), b16),
            pltpu.VMEM((chunks, CHUNK, rows), f32),
            pltpu.VMEM((chunks, CHUNK, rows), f32),
            pltpu.VMEM((chunks, 1, rows), f32),
            pltpu.VMEM((8, rows), f32),
            pltpu.VMEM((HD, rows), f32),
            pltpu.VMEM((rows, HD), f32),
            pltpu.VMEM((rows, HD), f32),
            pltpu.VMEM((2, rows, HD), f32),
        ],
        compiler_params=pltpu.CompilerParams(vmem_limit_bytes=62 * 1024 * 1024),
        name="attend",
    )(q, do, k, v, seg_cols, slots)


def scatter_kernel(terms_ref, out_ref, half, sums, got, pair_send, pair_recv, send_sem, recv_sem):
    chips = terms_ref.shape[0]
    me = lax.axis_index("ctx")
    chip = me // 2
    core = me % 2
    partner = {"ctx": 2 * chip + 1 - core}
    peer = lambda k: {"ctx": 2 * k + core}

    barrier = pltpu.get_barrier_semaphore()
    pl.semaphore_signal(barrier, inc=1, device_id=partner, device_id_type=MESH)

    def greet(k, _):
        pl.semaphore_signal(barrier, inc=1, device_id=peer(k), device_id_type=MESH)
        return 0

    lax.fori_loop(chip + 1, chips, greet, 0)
    pl.semaphore_wait(barrier, chip + 1)

    def pair_copy(j):
        return pltpu.make_async_remote_copy(
            src_ref=terms_ref.at[j, 1 - core],
            dst_ref=half.at[j],
            send_sem=pair_send.at[j],
            recv_sem=pair_recv.at[j],
            device_id=partner,
            device_id_type=MESH,
        )

    def send_copy(j, source):
        return pltpu.make_async_remote_copy(
            src_ref=sums.at[j],
            dst_ref=got.at[source],
            send_sem=send_sem.at[j],
            recv_sem=recv_sem.at[source],
            device_id=peer(j),
            device_id_type=MESH,
        )

    def start_pair(j, _):
        pair_copy(j).start()
        return 0

    lax.fori_loop(0, chip + 1, start_pair, 0)

    def pass_on(j, _):
        pair_copy(j).wait_recv()
        total = terms_ref[j, core].astype(jnp.float32) + half[j].astype(jnp.float32)
        sums[j] = total.astype(jnp.bfloat16)
        send_copy(j, chip).start()
        return 0

    lax.fori_loop(0, chip, pass_on, 0)
    pair_copy(chip).wait_recv()
    out_ref[...] = terms_ref[chip, core].astype(jnp.float32) + half[chip].astype(jnp.float32)

    def take(k, _):
        send_copy(k, k).wait_recv()
        out_ref[...] = out_ref[...] + got[k].astype(jnp.float32)
        return 0

    lax.fori_loop(chip + 1, chips, take, 0)

    def end_send(j, _):
        send_copy(j, chip).wait_send()
        return 0

    lax.fori_loop(0, chip, end_send, 0)

    def end_pair(j, _):
        pair_copy(j).wait_send()
        return 0

    lax.fori_loop(0, chip + 1, end_pair, 0)


def scatter(terms):
    total, wide = terms.shape
    chips = total // (2 * SLOT_DEV)
    block = (chips, SLOT_DEV, wide)
    vmem = pl.BlockSpec(memory_space=pltpu.VMEM)
    return pl.pallas_call(
        scatter_kernel,
        in_specs=[vmem],
        out_specs=vmem,
        out_shape=jax.ShapeDtypeStruct((SLOT_DEV, wide), jnp.float32),
        scratch_shapes=[
            pltpu.VMEM(block, jnp.bfloat16),
            pltpu.VMEM(block, jnp.bfloat16),
            pltpu.VMEM(block, jnp.bfloat16),
            pltpu.SemaphoreType.DMA((chips,)),
            pltpu.SemaphoreType.DMA((chips,)),
            pltpu.SemaphoreType.DMA((chips,)),
            pltpu.SemaphoreType.DMA((chips,)),
        ],
        compiler_params=pltpu.CompilerParams(collective_id=0, has_side_effects=True),
        name="scatter",
    )(terms.reshape(chips, 2, SLOT_DEV, wide))


def enter_kernel(
    q_ref, do_ref, k_ref, v_ref, seg_ref,
    qo_ref, doo_ref, ko_ref, vo_ref, slots_ref,
    kb, vb, mine, local_sem, x_send, x_recv, ag_send, ag_recv, pair_send, pair_recv,
):
    heads = lax.axis_size("head")
    chips = lax.axis_size("ctx") // 2
    chunk_chips = CHUNK_BLOCKS // 2
    part = q_ref.shape[0]
    head = lax.axis_index("head")
    me = lax.axis_index("ctx")
    chip = me // 2
    core = me % 2
    low = chunk_chips * (chip // chunk_chips)
    high = low + chunk_chips
    partner = {"ctx": 2 * chip + 1 - core}
    peer = lambda k: {"ctx": 2 * k + core}

    def others(first, last, body):
        def step(k, _):
            pl.when(k != chip)(lambda: body(k))
            return 0

        lax.fori_loop(first, last, step, 0)

    barrier = pltpu.get_barrier_semaphore()
    greet = lambda device: pl.semaphore_signal(barrier, inc=1, device_id=device, device_id_type=MESH)
    for d in range(1, heads):
        greet({"head": (head + d) % heads})
    greet(partner)
    others(0, high, lambda k: greet(peer(k)))
    pl.semaphore_wait(barrier, heads + chips - low - 1)

    pairs = ((k_ref, kb), (v_ref, vb), (q_ref, qo_ref), (do_ref, doo_ref))

    def span(n, target):
        source, landing = pairs[n]
        wide = source.shape[1] // heads
        columns = pl.ds(pl.multiple_of(target * wide, HD), wide)
        rows = pl.ds(pl.multiple_of(head * part, 16), part)
        return source.at[:, columns], landing.at[rows, :]

    def cross(n, d):
        target = (head + d) % heads
        source, landing = span(n, target)
        return pltpu.make_async_remote_copy(
            src_ref=source,
            dst_ref=landing,
            send_sem=x_send.at[d, n],
            recv_sem=x_recv.at[d, n],
            device_id={"head": target},
            device_id_type=MESH,
        )

    def keep(n):
        return pltpu.make_async_copy(*span(n, head), local_sem.at[n])

    for n in range(4):
        for d in range(1, heads):
            cross(n, d).start()
        keep(n).start()
    for n in range(2):
        for d in range(1, heads):
            cross(n, d).wait_recv()
        keep(n).wait()

    tokens = kb.shape[0]
    ko_ref[...] = kb[...]
    vo_ref[...] = vb[...]
    slot = lax.broadcasted_iota(jnp.int32, (SLOT_DEV, tokens), 0)
    for g in range(kb.shape[1] // HD):
        picks = (slot == seg_ref[g : g + 1, :]).astype(jnp.float32)
        counts = jnp.sum(picks, axis=1, keepdims=True)
        sizes = jnp.maximum(counts, 1.0)
        onehot = picks.astype(jnp.bfloat16)
        cut = slice(g * HD, (g + 1) * HD)
        keys = jnp.where(counts > 0, dot_nn(onehot, kb[:, cut]) / sizes, DEAD_KEY)
        values = dot_nn(onehot, vb[:, cut]) / sizes
        mine[:, 2 * g * HD : (2 * g + 1) * HD] = keys.astype(jnp.bfloat16)
        mine[:, (2 * g + 1) * HD : (2 * g + 2) * HD] = values.astype(jnp.bfloat16)

    def spread_copy(target, source):
        return pltpu.make_async_remote_copy(
            src_ref=mine,
            dst_ref=slots_ref.at[2 * source + core],
            send_sem=ag_send.at[target],
            recv_sem=ag_recv.at[source],
            device_id=peer(target),
            device_id_type=MESH,
        )

    def pair_copy(k, source):
        return pltpu.make_async_remote_copy(
            src_ref=source,
            dst_ref=slots_ref.at[2 * k + core],
            send_sem=pair_send.at[k],
            recv_sem=pair_recv.at[k],
            device_id=partner,
            device_id_type=MESH,
        )

    relay = lambda k: pair_copy(k, slots_ref.at[2 * k + core])
    arrive = lambda k: pltpu.make_async_remote_copy(
        src_ref=mine,
        dst_ref=slots_ref.at[2 * k + 1 - core],
        send_sem=pair_send.at[k],
        recv_sem=pair_recv.at[k],
        device_id=partner,
        device_id_type=MESH,
    )
    place = pltpu.make_async_copy(mine, slots_ref.at[me], local_sem.at[4])

    def start_spread(n, _):
        target = chips - 1 - n
        pl.when(target != chip)(lambda: spread_copy(target, chip).start())
        return 0

    lax.fori_loop(0, chips - low, start_spread, 0)
    pair_copy(chip, mine).start()
    place.start()

    def pass_on(k):
        spread_copy(k, k).wait_recv()
        relay(k).start()

    others(0, high, pass_on)
    place.wait()

    def end_pair(k, _):
        arrive(k).wait_recv()
        relay(k).wait_send()
        return 0

    lax.fori_loop(0, high, end_pair, 0)
    others(low, chips, lambda k: spread_copy(k, chip).wait_send())
    for n in range(2, 4):
        for d in range(1, heads):
            cross(n, d).wait_recv()
        keep(n).wait()
    for n in range(4):
        for d in range(1, heads):
            cross(n, d).wait_send()


def enter(q, do, k, v, seg):
    part, wide = q.shape
    narrow = k.shape[1]
    heads = lax.axis_size("head")
    shards = lax.axis_size("ctx")
    chips = shards // 2
    tokens = part * heads
    b16 = jnp.bfloat16
    vmem = pl.BlockSpec(memory_space=pltpu.VMEM)
    anywhere = pl.BlockSpec(memory_space=pl.ANY)
    dma = pltpu.SemaphoreType.DMA
    return pl.pallas_call(
        enter_kernel,
        in_specs=[vmem] * 5,
        out_specs=[anywhere, anywhere, vmem, vmem, anywhere],
        out_shape=[
            jax.ShapeDtypeStruct((tokens, wide // heads), b16),
            jax.ShapeDtypeStruct((tokens, wide // heads), b16),
            jax.ShapeDtypeStruct((tokens, narrow // heads), b16),
            jax.ShapeDtypeStruct((tokens, narrow // heads), b16),
            jax.ShapeDtypeStruct((shards, SLOT_DEV, 2 * narrow // heads), b16),
        ],
        scratch_shapes=[
            pltpu.VMEM((tokens, narrow // heads), b16),
            pltpu.VMEM((tokens, narrow // heads), b16),
            pltpu.VMEM((SLOT_DEV, 2 * narrow // heads), b16),
            dma((5,)),
            dma((heads, 4)),
            dma((heads, 4)),
            dma((chips,)),
            dma((chips,)),
            dma((chips,)),
            dma((chips,)),
        ],
        compiler_params=pltpu.CompilerParams(collective_id=1, has_side_effects=True),
        name="enter",
    )(q, do, k, v, seg)


def local(queries, keys, values, segment_ids, grad_out):
    queries, grad_out, keys, values, slots = enter(queries, grad_out, keys, values, segment_ids)
    tokens = queries.shape[0]
    kv_heads = keys.shape[1] // HD
    slot_picks = segment_ids[:, :, None] == jnp.arange(SLOT_DEV, dtype=jnp.int32)[None, None, :]
    counts = jnp.sum(slot_picks.astype(jnp.int32), axis=1)
    grad_queries, own_k, own_v, slot_terms = attend(
        queries, grad_out, keys, values, segment_ids[:, :, None], slots.reshape(-1, slots.shape[2])
    )
    slot_total = scatter(slot_terms).reshape(SLOT_DEV, kv_heads, 2, HD)
    slot_spread = jnp.einsum(
        "gts,sgcd->tgcd",
        slot_picks.astype(jnp.float32),
        slot_total,
        precision=lax.Precision.HIGHEST,
    )
    token_sizes = jnp.sum(jnp.where(slot_picks, counts[:, None, :], 0), axis=2).T.astype(jnp.float32)
    spread = lambda n, own: (
        slot_spread[:, :, n] / token_sizes[..., None] + own.reshape(tokens, kv_heads, HD)
    ).astype(jnp.bfloat16).reshape(tokens, kv_heads * HD)
    return grad_queries, spread(0, own_k), spread(1, own_v)


def solution(mesh):
    both = P(("ctx", "head"), None)
    return jax.shard_map(
        local,
        mesh=mesh,
        in_specs=(both, both, both, P("head", "ctx"), both),
        out_specs=(P("ctx", "head"), P("ctx", "head"), P("ctx", "head")),
        check_vma=False,
    )
```

```python
import jax
import jax.numpy as jnp
import numpy as np
from jax import lax
from jax.experimental import pallas as pl
from jax.experimental.pallas import tpu as pltpu
from jax.sharding import PartitionSpec as P

QH = 64
KVH = 8
HD = 128
SLOT_DEV = 96
GROUP = QH // KVH
CHUNK_BLOCKS = 4
CHUNK = CHUNK_BLOCKS * SLOT_DEV
ROW_TILE = 512
HIDDEN = -1e30
DEAD_KEY = 128.0
DEAD_TEST = 64.0
MESH = pl.DeviceIdType.MESH
SCALE = HD**-0.5
SCALE2 = SCALE * 1.4426950408889634


def dot_nt(a, b, **kw):
    return lax.dot_general(a, b, (((1,), (1,)), ((), ())), preferred_element_type=jnp.float32, **kw)


def dot_nn(a, b):
    return lax.dot_general(a, b, (((1,), (0,)), ((), ())), preferred_element_type=jnp.float32)


def attend_kernel(
    q_ref, do_ref, k_ref, v_ref, seg_ref, slots_ref,
    dq_ref, ownk_ref, ownv_ref, out_ref,
    qa, dor, ka, kt, e_s, gp_s, mc, st, dqt, qs, dos, cols,
    terms, half, sums, got, pair_send, pair_recv, send_sem, recv_sem,
):
    tokens = q_ref.shape[0]
    rows = GROUP * tokens
    own = lax.axis_index("ctx")
    chunks = own // CHUNK_BLOCKS + 1
    g = pl.program_id(0)
    heads, chips = terms.shape[:2]
    chip = own // 2
    core = own % 2
    chunk_chips = CHUNK_BLOCKS // 2
    partner = {"ctx": 2 * chip + 1 - core}
    peer = lambda k: {"ctx": 2 * k + core}
    barrier = pltpu.get_barrier_semaphore()

    @pl.when(g == 0)
    def _():
        pl.semaphore_signal(barrier, inc=1, device_id=partner, device_id_type=MESH)

        def greet(k, _):
            pl.semaphore_signal(barrier, inc=1, device_id=peer(k), device_id_type=MESH)
            return 0

        lax.fori_loop(chip + 1, chips, greet, 0)

    def pair_copy(n, j):
        return pltpu.make_async_remote_copy(
            src_ref=terms.at[n, j, 1 - core],
            dst_ref=half.at[n, j],
            send_sem=pair_send.at[n, j],
            recv_sem=pair_recv.at[n, j],
            device_id=partner,
            device_id_type=MESH,
        )

    def send_copy(n, j, source):
        return pltpu.make_async_remote_copy(
            src_ref=sums.at[n, j],
            dst_ref=got.at[n, source],
            send_sem=send_sem.at[n, j],
            recv_sem=recv_sem.at[n, source],
            device_id=peer(j),
            device_id_type=MESH,
        )

    def pair_sum(n, j):
        pair_copy(n, j).wait_recv()
        return terms[n, j, core].astype(jnp.float32) + half[n, j].astype(jnp.float32)

    def pass_on(n, c):
        def step(j, _):
            sums[n, j] = pair_sum(n, j).astype(jnp.bfloat16)
            send_copy(n, j, chip).start()
            return 0

        lax.fori_loop(chunk_chips * c, jnp.minimum(chunk_chips * (c + 1), chip), step, 0)

    slot = lax.broadcasted_iota(jnp.int32, (HD, tokens), 0)
    onehot = (slot == seg_ref[pl.ds(g, 1), :]).astype(jnp.float32).T.astype(jnp.bfloat16)
    for h in range(GROUP):
        part = pl.ds(h * tokens, tokens)
        qa[part, 0:HD] = q_ref[:, h * HD : (h + 1) * HD]
        qa[part, HD : 2 * HD] = onehot
        dor[part, :] = do_ref[:, h * HD : (h + 1) * HD]

    kf = k_ref[...].astype(jnp.float32)
    vf = v_ref[...].astype(jnp.float32)
    ones = jnp.ones((8, HD), jnp.float32)
    for h in range(GROUP):
        part = pl.ds(h * tokens, tokens)
        qs[part, :] = q_ref[:, h * HD : (h + 1) * HD].astype(jnp.float32) * kf
        dos[part, :] = do_ref[:, h * HD : (h + 1) * HD].astype(jnp.float32) * vf
    own_s = dot_nt(ones, qs[...], precision=lax.Precision.HIGHEST)[0:1] * SCALE2
    own_g = dot_nt(ones, dos[...], precision=lax.Precision.HIGHEST)[0:1]
    st[0:1, :] = own_s
    st[1:2, :] = own_g
    st[2:3, :] = own_s
    st[3:4, :] = jnp.ones_like(own_s)
    st[4:5, :] = own_g

    srow = lax.broadcasted_iota(jnp.int32, (SLOT_DEV, HD), 0)
    slane = lax.broadcasted_iota(jnp.int32, (SLOT_DEV, HD), 1)
    diag = jnp.where(srow >= slane, HIDDEN, 0.0)

    def stat_step(c, _):
        base = pl.multiple_of(c * CHUNK, CHUNK)
        keys = slots_ref[pl.ds(base, CHUNK), 0:HD]
        ka[:, 0:HD] = keys
        for b in range(CHUNK_BLOCKS):
            block = c * CHUNK_BLOCKS + b
            part = slice(b * SLOT_DEV, (b + 1) * SLOT_DEV)
            kb = keys[part].astype(jnp.float32)
            dead = jnp.where(kb > DEAD_TEST, HIDDEN, 0.0)
            bias = jnp.where(block == own, diag, jnp.where(block > own, HIDDEN, dead))
            ka[part, HD : 2 * HD] = bias.astype(jnp.bfloat16)
        kt[c] = keys.astype(jnp.float32).T.astype(jnp.bfloat16)
        aug = ka[...]
        values = slots_ref[pl.ds(base, CHUNK), HD : 2 * HD]
        for r in range(0, rows, ROW_TILE):
            cut = slice(r, r + ROW_TILE)
            s = dot_nt(aug, qa[cut, :])
            gp = dot_nt(values, dor[cut, :])
            m_old = st[2:3, cut]
            m_new = jnp.maximum(m_old, jnp.max(s, axis=0, keepdims=True) * SCALE2)
            e = jnp.exp2(s * SCALE2 - m_new)
            back = jnp.exp2(m_old - m_new)
            e_s[c, :, cut] = e
            gp_s[c, :, cut] = gp
            mc[c, :, cut] = m_new
            st[2:3, cut] = m_new
            st[3:4, cut] = st[3:4, cut] * back + jnp.sum(e, axis=0, keepdims=True)
            st[4:5, cut] = st[4:5, cut] * back + jnp.sum(e * gp, axis=0, keepdims=True)
        return 0

    lax.fori_loop(0, chunks, stat_step, 0)

    maxima = st[2:3, :]
    inverse = 1.0 / st[3:4, :]
    deltas = st[4:5, :] * inverse
    own_p = jnp.exp2(st[0:1, :] - maxima) * inverse
    own_gs = own_p * (st[1:2, :] - deltas) * SCALE
    st[5:6, :] = deltas
    st[6:7, :] = inverse * SCALE
    inv_c = jnp.broadcast_to(inverse, (HD, rows)).T
    cols[0] = jnp.broadcast_to(own_gs, (HD, rows)).T
    cols[1] = jnp.broadcast_to(own_p, (HD, rows)).T
    qs16 = (qa[:, 0:HD].astype(jnp.float32) * (inv_c * SCALE)).astype(jnp.bfloat16)
    dos16 = (dor[...].astype(jnp.float32) * inv_c).astype(jnp.bfloat16)
    dor[...] = dos16
    dqt[...] = jnp.zeros_like(dqt)

    own_k = jnp.zeros((tokens, HD), jnp.float32)
    own_v = jnp.zeros((tokens, HD), jnp.float32)
    for h in range(GROUP):
        part = pl.ds(h * tokens, tokens)
        own_k = own_k + cols[0, part, :] * q_ref[:, h * HD : (h + 1) * HD].astype(jnp.float32)
        own_v = own_v + cols[1, part, :] * do_ref[:, h * HD : (h + 1) * HD].astype(jnp.float32)
    ownk_ref[...] = own_k
    ownv_ref[...] = own_v
    qa[:, 0:HD] = qs16

    @pl.when(g == 0)
    def _():
        pl.semaphore_wait(barrier, chip + 1)

    def grad_step(c, _):
        key_t = kt[c]
        acc_k = jnp.zeros((CHUNK, HD), jnp.float32)
        acc_v = jnp.zeros((CHUNK, HD), jnp.float32)
        for r in range(0, rows, ROW_TILE):
            cut = slice(r, r + ROW_TILE)
            back = jnp.exp2(mc[c, :, cut] - st[2:3, cut])
            e = e_s[c, :, cut] * back
            ds = e * (gp_s[c, :, cut] - st[5:6, cut])
            e16 = e.astype(jnp.bfloat16)
            ds16 = ds.astype(jnp.bfloat16)
            acc_v = acc_v + dot_nn(e16, dor[cut, :])
            acc_k = acc_k + dot_nn(ds16, qa[cut, 0:HD])
            dqt[:, cut] = dqt[:, cut] + dot_nn(key_t, ds16)
        for b in range(CHUNK_BLOCKS):
            part = slice(b * SLOT_DEV, (b + 1) * SLOT_DEV)
            terms[g, chunk_chips * c + b // 2, b % 2, :, 0:HD] = acc_k[part].astype(jnp.bfloat16)
            terms[g, chunk_chips * c + b // 2, b % 2, :, HD : 2 * HD] = acc_v[part].astype(jnp.bfloat16)

        def swap(j, _):
            pair_copy(g, j).start()
            return 0

        lax.fori_loop(chunk_chips * c, jnp.minimum(chunk_chips * (c + 1), chip + 1), swap, 0)
        pl.when(c > 0)(lambda: pass_on(g, c - 1))
        return 0

    lax.fori_loop(0, chunks, grad_step, 0)
    pass_on(g, chunks - 1)

    kf = k_ref[...].astype(jnp.float32)
    for h in range(GROUP):
        cut = slice(h * tokens, (h + 1) * tokens)
        part = pl.ds(h * tokens, tokens)
        qs[part, :] = cols[0, part, :] * kf
    for r in range(0, rows, ROW_TILE):
        cut = slice(r, r + ROW_TILE)
        qs[cut, :] = qs[cut, :] + (dqt[:, cut] * st[6:7, cut]).T
    for h in range(GROUP):
        part = pl.ds(h * tokens, tokens)
        dq_ref[:, h * HD : (h + 1) * HD] = qs[part, :].astype(jnp.bfloat16)

    @pl.when(g == heads - 1)
    def _():
        for n in range(heads):
            cut = slice(2 * n * HD, 2 * (n + 1) * HD)
            out_ref[:, cut] = pair_sum(n, chip)

            def take(k, _):
                send_copy(n, k, k).wait_recv()
                out_ref[:, cut] = out_ref[:, cut] + got[n, k].astype(jnp.float32)
                return 0

            lax.fori_loop(chip + 1, chips, take, 0)

            def end_send(j, _):
                send_copy(n, j, chip).wait_send()
                return 0

            lax.fori_loop(0, chip, end_send, 0)

            def end_pair(j, _):
                pair_copy(n, j).wait_send()
                return 0

            lax.fori_loop(0, chip + 1, end_pair, 0)


def attend(q, do, k, v, seg, slots):
    tokens = q.shape[0]
    total = slots.shape[0]
    heads = k.shape[1] // HD
    rows = GROUP * tokens
    chunks = total // CHUNK
    wide = GROUP * HD
    by_head = lambda g: (0, g)
    f32, b16 = jnp.float32, jnp.bfloat16
    dma = pltpu.SemaphoreType.DMA
    chips = total // (2 * SLOT_DEV)
    block = (heads, chips, SLOT_DEV, 2 * HD)
    return pl.pallas_call(
        attend_kernel,
        grid=(heads,),
        in_specs=[
            pl.BlockSpec((tokens, wide), by_head),
            pl.BlockSpec((tokens, wide), by_head),
            pl.BlockSpec((tokens, HD), by_head),
            pl.BlockSpec((tokens, HD), by_head),
            pl.BlockSpec((heads, tokens), lambda g: (0, 0)),
            pl.BlockSpec((total, 2 * HD), by_head),
        ],
        out_specs=[
            pl.BlockSpec((tokens, wide), by_head),
            pl.BlockSpec((tokens, HD), by_head),
            pl.BlockSpec((tokens, HD), by_head),
            pl.BlockSpec((SLOT_DEV, 2 * heads * HD), lambda g: (0, 0)),
        ],
        out_shape=[
            jax.ShapeDtypeStruct(q.shape, b16),
            jax.ShapeDtypeStruct(k.shape, f32),
            jax.ShapeDtypeStruct(k.shape, f32),
            jax.ShapeDtypeStruct((SLOT_DEV, 2 * heads * HD), f32),
        ],
        scratch_shapes=[
            pltpu.VMEM((rows, 2 * HD), b16),
            pltpu.VMEM((rows, HD), b16),
            pltpu.VMEM((CHUNK, 2 * HD), b16),
            pltpu.VMEM((chunks, HD, CHUNK), b16),
            pltpu.VMEM((chunks, CHUNK, rows), f32),
            pltpu.VMEM((chunks, CHUNK, rows), f32),
            pltpu.VMEM((chunks, 1, rows), f32),
            pltpu.VMEM((8, rows), f32),
            pltpu.VMEM((HD, rows), f32),
            pltpu.VMEM((rows, HD), f32),
            pltpu.VMEM((rows, HD), f32),
            pltpu.VMEM((2, rows, HD), f32),
            pltpu.VMEM((heads, chips, 2, SLOT_DEV, 2 * HD), b16),
            pltpu.VMEM(block, b16),
            pltpu.VMEM(block, b16),
            pltpu.VMEM(block, b16),
            dma((heads, chips)),
            dma((heads, chips)),
            dma((heads, chips)),
            dma((heads, chips)),
        ],
        compiler_params=pltpu.CompilerParams(
            vmem_limit_bytes=63 * 1024 * 1024, collective_id=0, has_side_effects=True
        ),
        name="attend",
    )(q, do, k, v, seg, slots)


def enter_kernel(
    q_ref, do_ref, k_ref, v_ref, seg_ref,
    qo_ref, doo_ref, ko_ref, vo_ref, slots_ref,
    kb, vb, mine, local_sem, x_send, x_recv, ag_send, ag_recv, pair_send, pair_recv,
):
    heads = lax.axis_size("head")
    chips = lax.axis_size("ctx") // 2
    chunk_chips = CHUNK_BLOCKS // 2
    part = q_ref.shape[0]
    head = lax.axis_index("head")
    me = lax.axis_index("ctx")
    chip = me // 2
    core = me % 2
    low = chunk_chips * (chip // chunk_chips)
    high = low + chunk_chips
    partner = {"ctx": 2 * chip + 1 - core}
    peer = lambda k: {"ctx": 2 * k + core}

    def others(first, last, body):
        def step(k, _):
            pl.when(k != chip)(lambda: body(k))
            return 0

        lax.fori_loop(first, last, step, 0)

    barrier = pltpu.get_barrier_semaphore()
    greet = lambda device: pl.semaphore_signal(barrier, inc=1, device_id=device, device_id_type=MESH)
    for d in range(1, heads):
        greet({"head": (head + d) % heads})
    greet(partner)
    others(0, high, lambda k: greet(peer(k)))
    pl.semaphore_wait(barrier, heads + chips - low - 1)

    pairs = ((k_ref, kb), (v_ref, vb), (q_ref, qo_ref), (do_ref, doo_ref))

    def span(n, target):
        source, landing = pairs[n]
        wide = source.shape[1] // heads
        columns = pl.ds(pl.multiple_of(target * wide, HD), wide)
        rows = pl.ds(pl.multiple_of(head * part, 16), part)
        return source.at[:, columns], landing.at[rows, :]

    def cross(n, d):
        target = (head + d) % heads
        source, landing = span(n, target)
        return pltpu.make_async_remote_copy(
            src_ref=source,
            dst_ref=landing,
            send_sem=x_send.at[d, n],
            recv_sem=x_recv.at[d, n],
            device_id={"head": target},
            device_id_type=MESH,
        )

    def keep(n):
        return pltpu.make_async_copy(*span(n, head), local_sem.at[n])

    for n in range(4):
        for d in range(1, heads):
            cross(n, d).start()
        keep(n).start()
    for n in range(2):
        for d in range(1, heads):
            cross(n, d).wait_recv()
        keep(n).wait()

    tokens = kb.shape[0]
    ko_ref[...] = kb[...]
    vo_ref[...] = vb[...]
    slot = lax.broadcasted_iota(jnp.int32, (SLOT_DEV, tokens), 0)
    for g in range(kb.shape[1] // HD):
        picks = (slot == seg_ref[g : g + 1, :]).astype(jnp.float32)
        counts = jnp.sum(picks, axis=1, keepdims=True)
        sizes = jnp.maximum(counts, 1.0)
        onehot = picks.astype(jnp.bfloat16)
        cut = slice(g * HD, (g + 1) * HD)
        keys = jnp.where(counts > 0, dot_nn(onehot, kb[:, cut]) / sizes, DEAD_KEY)
        values = dot_nn(onehot, vb[:, cut]) / sizes
        mine[:, 2 * g * HD : (2 * g + 1) * HD] = keys.astype(jnp.bfloat16)
        mine[:, (2 * g + 1) * HD : (2 * g + 2) * HD] = values.astype(jnp.bfloat16)

    def spread_copy(target, source):
        return pltpu.make_async_remote_copy(
            src_ref=mine,
            dst_ref=slots_ref.at[2 * source + core],
            send_sem=ag_send.at[target],
            recv_sem=ag_recv.at[source],
            device_id=peer(target),
            device_id_type=MESH,
        )

    def pair_copy(k, source):
        return pltpu.make_async_remote_copy(
            src_ref=source,
            dst_ref=slots_ref.at[2 * k + core],
            send_sem=pair_send.at[k],
            recv_sem=pair_recv.at[k],
            device_id=partner,
            device_id_type=MESH,
        )

    relay = lambda k: pair_copy(k, slots_ref.at[2 * k + core])
    arrive = lambda k: pltpu.make_async_remote_copy(
        src_ref=mine,
        dst_ref=slots_ref.at[2 * k + 1 - core],
        send_sem=pair_send.at[k],
        recv_sem=pair_recv.at[k],
        device_id=partner,
        device_id_type=MESH,
    )
    place = pltpu.make_async_copy(mine, slots_ref.at[me], local_sem.at[4])

    def start_spread(n, _):
        target = chips - 1 - n
        pl.when(target != chip)(lambda: spread_copy(target, chip).start())
        return 0

    lax.fori_loop(0, chips - low, start_spread, 0)
    pair_copy(chip, mine).start()
    place.start()

    def pass_on(k):
        spread_copy(k, k).wait_recv()
        relay(k).start()

    others(0, high, pass_on)
    place.wait()

    def end_pair(k, _):
        arrive(k).wait_recv()
        relay(k).wait_send()
        return 0

    lax.fori_loop(0, high, end_pair, 0)
    others(low, chips, lambda k: spread_copy(k, chip).wait_send())
    for n in range(2, 4):
        for d in range(1, heads):
            cross(n, d).wait_recv()
        keep(n).wait()
    for n in range(4):
        for d in range(1, heads):
            cross(n, d).wait_send()


def enter(q, do, k, v, seg):
    part, wide = q.shape
    narrow = k.shape[1]
    heads = lax.axis_size("head")
    shards = lax.axis_size("ctx")
    chips = shards // 2
    tokens = part * heads
    b16 = jnp.bfloat16
    vmem = pl.BlockSpec(memory_space=pltpu.VMEM)
    anywhere = pl.BlockSpec(memory_space=pl.ANY)
    dma = pltpu.SemaphoreType.DMA
    return pl.pallas_call(
        enter_kernel,
        in_specs=[vmem] * 5,
        out_specs=[anywhere, anywhere, vmem, vmem, anywhere],
        out_shape=[
            jax.ShapeDtypeStruct((tokens, wide // heads), b16),
            jax.ShapeDtypeStruct((tokens, wide // heads), b16),
            jax.ShapeDtypeStruct((tokens, narrow // heads), b16),
            jax.ShapeDtypeStruct((tokens, narrow // heads), b16),
            jax.ShapeDtypeStruct((shards, SLOT_DEV, 2 * narrow // heads), b16),
        ],
        scratch_shapes=[
            pltpu.VMEM((tokens, narrow // heads), b16),
            pltpu.VMEM((tokens, narrow // heads), b16),
            pltpu.VMEM((SLOT_DEV, 2 * narrow // heads), b16),
            dma((5,)),
            dma((heads, 4)),
            dma((heads, 4)),
            dma((chips,)),
            dma((chips,)),
            dma((chips,)),
            dma((chips,)),
        ],
        compiler_params=pltpu.CompilerParams(collective_id=1, has_side_effects=True),
        name="enter",
    )(q, do, k, v, seg)


def local(queries, keys, values, segment_ids, grad_out):
    queries, grad_out, keys, values, slots = enter(queries, grad_out, keys, values, segment_ids)
    tokens = queries.shape[0]
    kv_heads = keys.shape[1] // HD
    slot_picks = segment_ids[:, :, None] == jnp.arange(SLOT_DEV, dtype=jnp.int32)[None, None, :]
    counts = jnp.sum(slot_picks.astype(jnp.int32), axis=1)
    grad_queries, own_k, own_v, slot_total = attend(
        queries, grad_out, keys, values, segment_ids, slots.reshape(-1, slots.shape[2])
    )
    slot_total = slot_total.reshape(SLOT_DEV, kv_heads, 2, HD)
    slot_spread = jnp.einsum(
        "gts,sgcd->tgcd",
        slot_picks.astype(jnp.float32),
        slot_total,
        precision=lax.Precision.HIGHEST,
    )
    token_sizes = jnp.sum(jnp.where(slot_picks, counts[:, None, :], 0), axis=2).T.astype(jnp.float32)
    spread = lambda n, own: (
        slot_spread[:, :, n] / token_sizes[..., None] + own.reshape(tokens, kv_heads, HD)
    ).astype(jnp.bfloat16).reshape(tokens, kv_heads * HD)
    return grad_queries, spread(0, own_k), spread(1, own_v)


def solution(mesh):
    both = P(("ctx", "head"), None)
    return jax.shard_map(
        local,
        mesh=mesh,
        in_specs=(both, both, both, P("head", "ctx"), both),
        out_specs=(P("ctx", "head"), P("ctx", "head"), P("ctx", "head")),
        check_vma=False,
    )
```

```python
import jax
import jax.numpy as jnp
import numpy as np
from jax import lax
from jax.experimental import pallas as pl
from jax.experimental.pallas import tpu as pltpu
from jax.sharding import PartitionSpec as P

QH = 64
KVH = 8
HD = 128
SLOT_DEV = 96
GROUP = QH // KVH
CHUNK_BLOCKS = 4
CHUNK = CHUNK_BLOCKS * SLOT_DEV
ROW_TILE = 512
HIDDEN = -1e30
DEAD_KEY = 128.0
DEAD_TEST = 64.0
MESH = pl.DeviceIdType.MESH
SCALE = HD**-0.5
SCALE2 = SCALE * 1.4426950408889634


def dot_nt(a, b, **kw):
    return lax.dot_general(a, b, (((1,), (1,)), ((), ())), preferred_element_type=jnp.float32, **kw)


def dot_nn(a, b):
    return lax.dot_general(a, b, (((1,), (0,)), ((), ())), preferred_element_type=jnp.float32)


def attend_kernel(
    q_ref, do_ref, k_ref, v_ref, seg_ref, slots_ref,
    dq_ref, ownk_ref, ownv_ref, out_ref,
    qa, dor, ka, kt, e_s, gp_s, mc, st, dqt, qs, dos, cols,
    terms, half, sums, got, pair_send, pair_recv, send_sem, recv_sem,
):
    tokens = q_ref.shape[0]
    rows = GROUP * tokens
    own = lax.axis_index("ctx")
    chunks = own // CHUNK_BLOCKS + 1
    g = pl.program_id(0)
    heads, chips = terms.shape[:2]
    chip = own // 2
    core = own % 2
    chunk_chips = CHUNK_BLOCKS // 2
    partner = {"ctx": 2 * chip + 1 - core}
    peer = lambda k: {"ctx": 2 * k + core}
    barrier = pltpu.get_barrier_semaphore()

    @pl.when(g == 0)
    def _():
        pl.semaphore_signal(barrier, inc=1, device_id=partner, device_id_type=MESH)

        def greet(k, _):
            pl.semaphore_signal(barrier, inc=1, device_id=peer(k), device_id_type=MESH)
            return 0

        lax.fori_loop(chip + 1, chips, greet, 0)

    def pair_copy(n, j):
        return pltpu.make_async_remote_copy(
            src_ref=terms.at[n, j, 1 - core],
            dst_ref=half.at[n, j],
            send_sem=pair_send.at[n, j],
            recv_sem=pair_recv.at[n, j],
            device_id=partner,
            device_id_type=MESH,
        )

    def send_copy(n, j, source):
        return pltpu.make_async_remote_copy(
            src_ref=sums.at[n, j],
            dst_ref=got.at[n, source],
            send_sem=send_sem.at[n, j],
            recv_sem=recv_sem.at[n, source],
            device_id=peer(j),
            device_id_type=MESH,
        )

    def pair_sum(n, j):
        pair_copy(n, j).wait_recv()
        return terms[n, j, core].astype(jnp.float32) + half[n, j].astype(jnp.float32)

    def pass_on(n, c):
        def step(j, _):
            sums[n, j] = pair_sum(n, j).astype(jnp.bfloat16)
            send_copy(n, j, chip).start()
            return 0

        lax.fori_loop(chunk_chips * c, jnp.minimum(chunk_chips * (c + 1), chip), step, 0)

    slot = lax.broadcasted_iota(jnp.int32, (HD, tokens), 0)
    onehot = (slot == seg_ref[pl.ds(g, 1), :]).astype(jnp.float32).T.astype(jnp.bfloat16)
    for h in range(GROUP):
        part = pl.ds(h * tokens, tokens)
        qa[part, 0:HD] = q_ref[:, h * HD : (h + 1) * HD]
        qa[part, HD : 2 * HD] = onehot
        dor[part, :] = do_ref[:, h * HD : (h + 1) * HD]

    kf = k_ref[...].astype(jnp.float32)
    vf = v_ref[...].astype(jnp.float32)
    ones = jnp.ones((8, HD), jnp.float32)
    for h in range(GROUP):
        part = pl.ds(h * tokens, tokens)
        qs[part, :] = q_ref[:, h * HD : (h + 1) * HD].astype(jnp.float32) * kf
        dos[part, :] = do_ref[:, h * HD : (h + 1) * HD].astype(jnp.float32) * vf
    own_s = dot_nt(ones, qs[...], precision=lax.Precision.HIGHEST)[0:1] * SCALE2
    own_g = dot_nt(ones, dos[...], precision=lax.Precision.HIGHEST)[0:1]
    st[0:1, :] = own_s
    st[1:2, :] = own_g
    st[2:3, :] = own_s
    st[3:4, :] = jnp.ones_like(own_s)
    st[4:5, :] = own_g

    srow = lax.broadcasted_iota(jnp.int32, (SLOT_DEV, HD), 0)
    slane = lax.broadcasted_iota(jnp.int32, (SLOT_DEV, HD), 1)
    diag = jnp.where(srow >= slane, HIDDEN, 0.0)

    def stat_step(c, _):
        base = pl.multiple_of(c * CHUNK, CHUNK)
        keys = slots_ref[pl.ds(base, CHUNK), 0:HD]
        ka[:, 0:HD] = keys
        for b in range(CHUNK_BLOCKS):
            block = c * CHUNK_BLOCKS + b
            part = slice(b * SLOT_DEV, (b + 1) * SLOT_DEV)
            kb = keys[part].astype(jnp.float32)
            dead = jnp.where(kb > DEAD_TEST, HIDDEN, 0.0)
            bias = jnp.where(block == own, diag, jnp.where(block > own, HIDDEN, dead))
            ka[part, HD : 2 * HD] = bias.astype(jnp.bfloat16)
        kt[c] = keys.astype(jnp.float32).T.astype(jnp.bfloat16)
        aug = ka[...]
        values = slots_ref[pl.ds(base, CHUNK), HD : 2 * HD]
        for r in range(0, rows, ROW_TILE):
            cut = slice(r, r + ROW_TILE)
            s = dot_nt(aug, qa[cut, :])
            gp = dot_nt(values, dor[cut, :])
            m_old = st[2:3, cut]
            m_new = jnp.maximum(m_old, jnp.max(s, axis=0, keepdims=True) * SCALE2)
            e = jnp.exp2(s * SCALE2 - m_new)
            back = jnp.exp2(m_old - m_new)
            e_s[c, :, cut] = e
            gp_s[c, :, cut] = gp
            mc[c, :, cut] = m_new
            st[2:3, cut] = m_new
            st[3:4, cut] = st[3:4, cut] * back + jnp.sum(e, axis=0, keepdims=True)
            st[4:5, cut] = st[4:5, cut] * back + jnp.sum(e * gp, axis=0, keepdims=True)
        return 0

    lax.fori_loop(0, chunks, stat_step, 0)

    maxima = st[2:3, :]
    inverse = 1.0 / st[3:4, :]
    deltas = st[4:5, :] * inverse
    own_p = jnp.exp2(st[0:1, :] - maxima) * inverse
    own_gs = own_p * (st[1:2, :] - deltas) * SCALE
    st[5:6, :] = deltas
    st[6:7, :] = inverse * SCALE
    inv_c = jnp.broadcast_to(inverse, (HD, rows)).T
    cols[0] = jnp.broadcast_to(own_gs, (HD, rows)).T
    cols[1] = jnp.broadcast_to(own_p, (HD, rows)).T
    qs16 = (qa[:, 0:HD].astype(jnp.float32) * (inv_c * SCALE)).astype(jnp.bfloat16)
    dos16 = (dor[...].astype(jnp.float32) * inv_c).astype(jnp.bfloat16)
    dor[...] = dos16
    dqt[...] = jnp.zeros_like(dqt)

    own_k = jnp.zeros((tokens, HD), jnp.float32)
    own_v = jnp.zeros((tokens, HD), jnp.float32)
    for h in range(GROUP):
        part = pl.ds(h * tokens, tokens)
        own_k = own_k + cols[0, part, :] * q_ref[:, h * HD : (h + 1) * HD].astype(jnp.float32)
        own_v = own_v + cols[1, part, :] * do_ref[:, h * HD : (h + 1) * HD].astype(jnp.float32)
    ownk_ref[...] = own_k
    ownv_ref[...] = own_v
    qa[:, 0:HD] = qs16

    @pl.when(g == 0)
    def _():
        pl.semaphore_wait(barrier, chip + 1)

    def grad_step(c, _):
        key_t = kt[c]
        acc_k = jnp.zeros((CHUNK, HD), jnp.float32)
        acc_v = jnp.zeros((CHUNK, HD), jnp.float32)
        for r in range(0, rows, ROW_TILE):
            cut = slice(r, r + ROW_TILE)
            back = jnp.exp2(mc[c, :, cut] - st[2:3, cut])
            e = e_s[c, :, cut] * back
            ds = e * (gp_s[c, :, cut] - st[5:6, cut])
            e16 = e.astype(jnp.bfloat16)
            ds16 = ds.astype(jnp.bfloat16)
            acc_v = acc_v + dot_nn(e16, dor[cut, :])
            acc_k = acc_k + dot_nn(ds16, qa[cut, 0:HD])
            dqt[:, cut] = dqt[:, cut] + dot_nn(key_t, ds16)
        for b in range(CHUNK_BLOCKS):
            part = slice(b * SLOT_DEV, (b + 1) * SLOT_DEV)
            terms[g, chunk_chips * c + b // 2, b % 2, :, 0:HD] = acc_k[part].astype(jnp.bfloat16)
            terms[g, chunk_chips * c + b // 2, b % 2, :, HD : 2 * HD] = acc_v[part].astype(jnp.bfloat16)

        def swap(j, _):
            pair_copy(g, j).start()
            return 0

        lax.fori_loop(chunk_chips * c, jnp.minimum(chunk_chips * (c + 1), chip + 1), swap, 0)
        pl.when(c > 0)(lambda: pass_on(g, c - 1))
        return 0

    lax.fori_loop(0, chunks, grad_step, 0)
    pass_on(g, chunks - 1)

    kf = k_ref[...].astype(jnp.float32)
    for h in range(GROUP):
        cut = slice(h * tokens, (h + 1) * tokens)
        part = pl.ds(h * tokens, tokens)
        qs[part, :] = cols[0, part, :] * kf
    for r in range(0, rows, ROW_TILE):
        cut = slice(r, r + ROW_TILE)
        qs[cut, :] = qs[cut, :] + (dqt[:, cut] * st[6:7, cut]).T
    for h in range(GROUP):
        part = pl.ds(h * tokens, tokens)
        dq_ref[:, h * HD : (h + 1) * HD] = qs[part, :].astype(jnp.bfloat16)

    @pl.when(g == heads - 1)
    def _():
        for n in range(heads):
            cut = slice(2 * n * HD, 2 * (n + 1) * HD)
            out_ref[:, cut] = pair_sum(n, chip)

            def take(k, _):
                send_copy(n, k, k).wait_recv()
                out_ref[:, cut] = out_ref[:, cut] + got[n, k].astype(jnp.float32)
                return 0

            lax.fori_loop(chip + 1, chips, take, 0)

            def end_send(j, _):
                send_copy(n, j, chip).wait_send()
                return 0

            lax.fori_loop(0, chip, end_send, 0)

            def end_pair(j, _):
                pair_copy(n, j).wait_send()
                return 0

            lax.fori_loop(0, chip + 1, end_pair, 0)


def attend(q, do, k, v, seg, slots):
    tokens = q.shape[0]
    total = slots.shape[0]
    heads = k.shape[1] // HD
    rows = GROUP * tokens
    chunks = total // CHUNK
    wide = GROUP * HD
    by_head = lambda g: (0, g)
    f32, b16 = jnp.float32, jnp.bfloat16
    dma = pltpu.SemaphoreType.DMA
    chips = total // (2 * SLOT_DEV)
    block = (heads, chips, SLOT_DEV, 2 * HD)
    return pl.pallas_call(
        attend_kernel,
        grid=(heads,),
        in_specs=[
            pl.BlockSpec((tokens, wide), by_head),
            pl.BlockSpec((tokens, wide), by_head),
            pl.BlockSpec((tokens, HD), by_head),
            pl.BlockSpec((tokens, HD), by_head),
            pl.BlockSpec((heads, tokens), lambda g: (0, 0)),
            pl.BlockSpec((total, 2 * HD), by_head),
        ],
        out_specs=[
            pl.BlockSpec((tokens, wide), by_head),
            pl.BlockSpec((tokens, HD), by_head),
            pl.BlockSpec((tokens, HD), by_head),
            pl.BlockSpec((SLOT_DEV, 2 * heads * HD), lambda g: (0, 0)),
        ],
        out_shape=[
            jax.ShapeDtypeStruct(q.shape, b16),
            jax.ShapeDtypeStruct(k.shape, f32),
            jax.ShapeDtypeStruct(k.shape, f32),
            jax.ShapeDtypeStruct((SLOT_DEV, 2 * heads * HD), f32),
        ],
        scratch_shapes=[
            pltpu.VMEM((rows, 2 * HD), b16),
            pltpu.VMEM((rows, HD), b16),
            pltpu.VMEM((CHUNK, 2 * HD), b16),
            pltpu.VMEM((chunks, HD, CHUNK), b16),
            pltpu.VMEM((chunks, CHUNK, rows), f32),
            pltpu.VMEM((chunks, CHUNK, rows), f32),
            pltpu.VMEM((chunks, 1, rows), f32),
            pltpu.VMEM((8, rows), f32),
            pltpu.VMEM((HD, rows), f32),
            pltpu.VMEM((rows, HD), f32),
            pltpu.VMEM((rows, HD), f32),
            pltpu.VMEM((2, rows, HD), f32),
            pltpu.VMEM((heads, chips, 2, SLOT_DEV, 2 * HD), b16),
            pltpu.VMEM(block, b16),
            pltpu.VMEM(block, b16),
            pltpu.VMEM(block, b16),
            dma((heads, chips)),
            dma((heads, chips)),
            dma((heads, chips)),
            dma((heads, chips)),
        ],
        compiler_params=pltpu.CompilerParams(
            vmem_limit_bytes=63 * 1024 * 1024, collective_id=0, has_side_effects=True
        ),
        name="attend",
    )(q, do, k, v, seg, slots)


def enter_kernel(
    q_ref, do_ref, k_ref, v_ref, seg_ref,
    qo_ref, doo_ref, ko_ref, vo_ref, slots_ref,
    kb, vb, mine, stage, local_sem, x_send, x_recv, far_send, far_recv, ag_send, ag_recv, pair_send, pair_recv,
):
    heads = lax.axis_size("head")
    chips = lax.axis_size("ctx") // 2
    chunk_chips = CHUNK_BLOCKS // 2
    part = q_ref.shape[0]
    head = lax.axis_index("head")
    me = lax.axis_index("ctx")
    chip = me // 2
    core = me % 2
    low = chunk_chips * (chip // chunk_chips)
    high = low + chunk_chips
    partner = {"ctx": 2 * chip + 1 - core}
    peer = lambda k: {"ctx": 2 * k + core}

    def others(first, last, body):
        def step(k, _):
            pl.when(k != chip)(lambda: body(k))
            return 0

        lax.fori_loop(first, last, step, 0)

    barrier = pltpu.get_barrier_semaphore()
    greet = lambda device: pl.semaphore_signal(barrier, inc=1, device_id=device, device_id_type=MESH)
    for d in range(1, heads):
        greet({"head": (head + d) % heads})
    greet(partner)
    others(0, high, lambda k: greet(peer(k)))
    pl.semaphore_wait(barrier, heads + chips - low - 1)

    pairs = ((k_ref, kb), (v_ref, vb), (q_ref, qo_ref), (do_ref, doo_ref))

    def span(n, target):
        source, landing = pairs[n]
        wide = source.shape[1] // heads
        columns = pl.ds(pl.multiple_of(target * wide, HD), wide)
        rows = pl.ds(pl.multiple_of(head * part, 16), part)
        return source.at[:, columns], landing.at[rows, :]

    def cross(n, d):
        target = (head + d) % heads
        source, landing = span(n, target)
        return pltpu.make_async_remote_copy(
            src_ref=source,
            dst_ref=landing,
            send_sem=x_send.at[d, n],
            recv_sem=x_recv.at[d, n],
            device_id={"head": target},
            device_id_type=MESH,
        )

    def keep(n):
        return pltpu.make_async_copy(*span(n, head), local_sem.at[n])

    def far_out(n):
        way = 1 if n == 2 else heads - 1
        return pltpu.make_async_remote_copy(
            src_ref=span(n, (head + 2) % heads)[0],
            dst_ref=stage.at[n - 2],
            send_sem=far_send.at[n - 2],
            recv_sem=far_recv.at[n - 2],
            device_id={"head": (head + way) % heads},
            device_id_type=MESH,
        )

    def far_on(n):
        way = 1 if n == 2 else heads - 1
        rows = pl.ds(pl.multiple_of((head + heads - way) % heads * part, 16), part)
        return pltpu.make_async_remote_copy(
            src_ref=stage.at[n - 2],
            dst_ref=pairs[n][1].at[rows, :],
            send_sem=x_send.at[2, n],
            recv_sem=x_recv.at[2, n],
            device_id={"head": (head + way) % heads},
            device_id_type=MESH,
        )

    for n in range(2):
        for d in range(1, heads):
            cross(n, d).start()
        keep(n).start()
    for n in range(2, 4):
        far_out(n).start()
    for n in range(2, 4):
        for d in (1, 3):
            cross(n, d).start()
        keep(n).start()
    for n in range(2):
        for d in range(1, heads):
            cross(n, d).wait_recv()
        keep(n).wait()

    tokens = kb.shape[0]
    ko_ref[...] = kb[...]
    vo_ref[...] = vb[...]
    slot = lax.broadcasted_iota(jnp.int32, (SLOT_DEV, tokens), 0)
    for g in range(kb.shape[1] // HD):
        picks = (slot == seg_ref[g : g + 1, :]).astype(jnp.float32)
        counts = jnp.sum(picks, axis=1, keepdims=True)
        sizes = jnp.maximum(counts, 1.0)
        onehot = picks.astype(jnp.bfloat16)
        cut = slice(g * HD, (g + 1) * HD)
        keys = jnp.where(counts > 0, dot_nn(onehot, kb[:, cut]) / sizes, DEAD_KEY)
        values = dot_nn(onehot, vb[:, cut]) / sizes
        mine[:, 2 * g * HD : (2 * g + 1) * HD] = keys.astype(jnp.bfloat16)
        mine[:, (2 * g + 1) * HD : (2 * g + 2) * HD] = values.astype(jnp.bfloat16)

    def spread_copy(target, source):
        return pltpu.make_async_remote_copy(
            src_ref=mine,
            dst_ref=slots_ref.at[2 * source + core],
            send_sem=ag_send.at[target],
            recv_sem=ag_recv.at[source],
            device_id=peer(target),
            device_id_type=MESH,
        )

    def pair_copy(k, source):
        return pltpu.make_async_remote_copy(
            src_ref=source,
            dst_ref=slots_ref.at[2 * k + core],
            send_sem=pair_send.at[k],
            recv_sem=pair_recv.at[k],
            device_id=partner,
            device_id_type=MESH,
        )

    relay = lambda k: pair_copy(k, slots_ref.at[2 * k + core])
    arrive = lambda k: pltpu.make_async_remote_copy(
        src_ref=mine,
        dst_ref=slots_ref.at[2 * k + 1 - core],
        send_sem=pair_send.at[k],
        recv_sem=pair_recv.at[k],
        device_id=partner,
        device_id_type=MESH,
    )
    place = pltpu.make_async_copy(mine, slots_ref.at[me], local_sem.at[4])

    def start_spread(n, _):
        target = chips - 1 - n
        pl.when(target != chip)(lambda: spread_copy(target, chip).start())
        return 0

    lax.fori_loop(0, chips - low, start_spread, 0)
    for n in range(2, 4):
        far_out(n).wait_recv()
        far_on(n).start()
    pair_copy(chip, mine).start()
    place.start()

    def pass_on(k):
        spread_copy(k, k).wait_recv()
        relay(k).start()

    others(0, high, pass_on)
    place.wait()

    def end_pair(k, _):
        arrive(k).wait_recv()
        relay(k).wait_send()
        return 0

    lax.fori_loop(0, high, end_pair, 0)
    others(low, chips, lambda k: spread_copy(k, chip).wait_send())
    for n in range(2, 4):
        for d in range(1, heads):
            cross(n, d).wait_recv()
        keep(n).wait()
        far_out(n).wait_send()
        far_on(n).wait_send()
    for n in range(4):
        for d in range(1, heads):
            if n < 2 or d != 2:
                cross(n, d).wait_send()


def enter(q, do, k, v, seg):
    part, wide = q.shape
    narrow = k.shape[1]
    heads = lax.axis_size("head")
    shards = lax.axis_size("ctx")
    chips = shards // 2
    tokens = part * heads
    b16 = jnp.bfloat16
    vmem = pl.BlockSpec(memory_space=pltpu.VMEM)
    anywhere = pl.BlockSpec(memory_space=pl.ANY)
    dma = pltpu.SemaphoreType.DMA
    return pl.pallas_call(
        enter_kernel,
        in_specs=[vmem] * 5,
        out_specs=[anywhere, anywhere, vmem, vmem, anywhere],
        out_shape=[
            jax.ShapeDtypeStruct((tokens, wide // heads), b16),
            jax.ShapeDtypeStruct((tokens, wide // heads), b16),
            jax.ShapeDtypeStruct((tokens, narrow // heads), b16),
            jax.ShapeDtypeStruct((tokens, narrow // heads), b16),
            jax.ShapeDtypeStruct((shards, SLOT_DEV, 2 * narrow // heads), b16),
        ],
        scratch_shapes=[
            pltpu.VMEM((tokens, narrow // heads), b16),
            pltpu.VMEM((tokens, narrow // heads), b16),
            pltpu.VMEM((SLOT_DEV, 2 * narrow // heads), b16),
            pltpu.VMEM((2, part, wide // heads), b16),
            dma((5,)),
            dma((heads, 4)),
            dma((heads, 4)),
            dma((2,)),
            dma((2,)),
            dma((chips,)),
            dma((chips,)),
            dma((chips,)),
            dma((chips,)),
        ],
        compiler_params=pltpu.CompilerParams(collective_id=1, has_side_effects=True),
        name="enter",
    )(q, do, k, v, seg)


def local(queries, keys, values, segment_ids, grad_out):
    queries, grad_out, keys, values, slots = enter(queries, grad_out, keys, values, segment_ids)
    tokens = queries.shape[0]
    kv_heads = keys.shape[1] // HD
    slot_picks = segment_ids[:, :, None] == jnp.arange(SLOT_DEV, dtype=jnp.int32)[None, None, :]
    counts = jnp.sum(slot_picks.astype(jnp.int32), axis=1)
    grad_queries, own_k, own_v, slot_total = attend(
        queries, grad_out, keys, values, segment_ids, slots.reshape(-1, slots.shape[2])
    )
    slot_total = slot_total.reshape(SLOT_DEV, kv_heads, 2, HD)
    slot_spread = jnp.einsum(
        "gts,sgcd->tgcd",
        slot_picks.astype(jnp.float32),
        slot_total,
        precision=lax.Precision.HIGHEST,
    )
    token_sizes = jnp.sum(jnp.where(slot_picks, counts[:, None, :], 0), axis=2).T.astype(jnp.float32)
    spread = lambda n, own: (
        slot_spread[:, :, n] / token_sizes[..., None] + own.reshape(tokens, kv_heads, HD)
    ).astype(jnp.bfloat16).reshape(tokens, kv_heads * HD)
    return grad_queries, spread(0, own_k), spread(1, own_v)


def solution(mesh):
    both = P(("ctx", "head"), None)
    return jax.shard_map(
        local,
        mesh=mesh,
        in_specs=(both, both, both, P("head", "ctx"), both),
        out_specs=(P("ctx", "head"), P("ctx", "head"), P("ctx", "head")),
        check_vma=False,
    )
```

```python
import jax
import jax.numpy as jnp
import numpy as np
from jax import lax
from jax.experimental import pallas as pl
from jax.experimental.pallas import tpu as pltpu
from jax.sharding import PartitionSpec as P

QH = 64
KVH = 8
HD = 128
SLOT_DEV = 96
GROUP = QH // KVH
CHUNK_BLOCKS = 4
CHUNK = CHUNK_BLOCKS * SLOT_DEV
ROW_TILE = 512
HIDDEN = -1e30
DEAD_KEY = 128.0
DEAD_TEST = 64.0
MESH = pl.DeviceIdType.MESH
SCALE = HD**-0.5
SCALE2 = SCALE * 1.4426950408889634


def dot_nt(a, b, **kw):
    return lax.dot_general(a, b, (((1,), (1,)), ((), ())), preferred_element_type=jnp.float32, **kw)


def dot_nn(a, b):
    return lax.dot_general(a, b, (((1,), (0,)), ((), ())), preferred_element_type=jnp.float32)


def attend_kernel(
    q_ref, do_ref, k_ref, v_ref, seg_ref, slots_ref,
    dq_ref, ownk_ref, ownv_ref, out_ref,
    qa, dor, ka, kt, e_s, gp_s, mc, st, dqt, qs, dos, cols,
    terms, half, sums, got, pair_send, pair_recv, send_sem, recv_sem,
):
    tokens = q_ref.shape[0]
    rows = GROUP * tokens
    own = lax.axis_index("ctx")
    chunks = own // CHUNK_BLOCKS + 1
    g = pl.program_id(0)
    heads, chips = terms.shape[:2]
    chip = own // 2
    core = own % 2
    chunk_chips = CHUNK_BLOCKS // 2
    partner = {"ctx": 2 * chip + 1 - core}
    peer = lambda k: {"ctx": 2 * k + core}
    barrier = pltpu.get_barrier_semaphore()

    @pl.when(g == 0)
    def _():
        pl.semaphore_signal(barrier, inc=1, device_id=partner, device_id_type=MESH)

        def greet(k, _):
            pl.semaphore_signal(barrier, inc=1, device_id=peer(k), device_id_type=MESH)
            return 0

        lax.fori_loop(chip + 1, chips, greet, 0)

    def pair_copy(n, j):
        return pltpu.make_async_remote_copy(
            src_ref=terms.at[n, j, 1 - core],
            dst_ref=half.at[n, j],
            send_sem=pair_send.at[n, j],
            recv_sem=pair_recv.at[n, j],
            device_id=partner,
            device_id_type=MESH,
        )

    def send_copy(n, j, source):
        return pltpu.make_async_remote_copy(
            src_ref=sums.at[n, j],
            dst_ref=got.at[n, source],
            send_sem=send_sem.at[n, j],
            recv_sem=recv_sem.at[n, source],
            device_id=peer(j),
            device_id_type=MESH,
        )

    def pair_sum(n, j):
        pair_copy(n, j).wait_recv()
        return terms[n, j, core].astype(jnp.float32) + half[n, j].astype(jnp.float32)

    def pass_on(n, c):
        def step(j, _):
            sums[n, j] = pair_sum(n, j).astype(jnp.bfloat16)
            send_copy(n, j, chip).start()
            return 0

        lax.fori_loop(chunk_chips * c, jnp.minimum(chunk_chips * (c + 1), chip), step, 0)

    slot = lax.broadcasted_iota(jnp.int32, (HD, tokens), 0)
    onehot = (slot == seg_ref[pl.ds(g, 1), :]).astype(jnp.float32).T.astype(jnp.bfloat16)
    for h in range(GROUP):
        part = pl.ds(h * tokens, tokens)
        qa[part, 0:HD] = q_ref[:, h * HD : (h + 1) * HD]
        qa[part, HD : 2 * HD] = onehot
        dor[part, :] = do_ref[:, h * HD : (h + 1) * HD]

    kf = k_ref[...].astype(jnp.float32)
    vf = v_ref[...].astype(jnp.float32)
    ones = jnp.ones((8, HD), jnp.float32)
    for h in range(GROUP):
        part = pl.ds(h * tokens, tokens)
        qs[part, :] = q_ref[:, h * HD : (h + 1) * HD].astype(jnp.float32) * kf
        dos[part, :] = do_ref[:, h * HD : (h + 1) * HD].astype(jnp.float32) * vf
    own_s = dot_nt(ones, qs[...], precision=lax.Precision.HIGHEST)[0:1] * SCALE2
    own_g = dot_nt(ones, dos[...], precision=lax.Precision.HIGHEST)[0:1]
    st[0:1, :] = own_s
    st[1:2, :] = own_g
    st[2:3, :] = own_s
    st[3:4, :] = jnp.ones_like(own_s)
    st[4:5, :] = own_g

    srow = lax.broadcasted_iota(jnp.int32, (SLOT_DEV, HD), 0)
    slane = lax.broadcasted_iota(jnp.int32, (SLOT_DEV, HD), 1)
    diag = jnp.where(srow >= slane, HIDDEN, 0.0)

    def stat_step(c, _):
        base = pl.multiple_of(c * CHUNK, CHUNK)
        keys = slots_ref[pl.ds(base, CHUNK), 0:HD]
        ka[:, 0:HD] = keys
        for b in range(CHUNK_BLOCKS):
            block = c * CHUNK_BLOCKS + b
            part = slice(b * SLOT_DEV, (b + 1) * SLOT_DEV)
            kb = keys[part].astype(jnp.float32)
            dead = jnp.where(kb > DEAD_TEST, HIDDEN, 0.0)
            bias = jnp.where(block == own, diag, jnp.where(block > own, HIDDEN, dead))
            ka[part, HD : 2 * HD] = bias.astype(jnp.bfloat16)
        kt[c] = keys.astype(jnp.float32).T.astype(jnp.bfloat16)
        aug = ka[...]
        values = slots_ref[pl.ds(base, CHUNK), HD : 2 * HD]
        for r in range(0, rows, ROW_TILE):
            cut = slice(r, r + ROW_TILE)
            s = dot_nt(aug, qa[cut, :])
            gp = dot_nt(values, dor[cut, :])
            m_old = st[2:3, cut]
            m_new = jnp.maximum(m_old, jnp.max(s, axis=0, keepdims=True) * SCALE2)
            e = jnp.exp2(s * SCALE2 - m_new)
            back = jnp.exp2(m_old - m_new)
            e_s[c, :, cut] = e
            gp_s[c, :, cut] = gp
            mc[c, :, cut] = m_new
            st[2:3, cut] = m_new
            st[3:4, cut] = st[3:4, cut] * back + jnp.sum(e, axis=0, keepdims=True)
            st[4:5, cut] = st[4:5, cut] * back + jnp.sum(e * gp, axis=0, keepdims=True)
        return 0

    lax.fori_loop(0, chunks, stat_step, 0)

    maxima = st[2:3, :]
    inverse = 1.0 / st[3:4, :]
    deltas = st[4:5, :] * inverse
    own_p = jnp.exp2(st[0:1, :] - maxima) * inverse
    own_gs = own_p * (st[1:2, :] - deltas) * SCALE
    st[5:6, :] = deltas
    st[6:7, :] = inverse * SCALE
    inv_c = jnp.broadcast_to(inverse, (HD, rows)).T
    cols[0] = jnp.broadcast_to(own_gs, (HD, rows)).T
    cols[1] = jnp.broadcast_to(own_p, (HD, rows)).T
    qs16 = (qa[:, 0:HD].astype(jnp.float32) * (inv_c * SCALE)).astype(jnp.bfloat16)
    dos16 = (dor[...].astype(jnp.float32) * inv_c).astype(jnp.bfloat16)
    dor[...] = dos16
    dqt[...] = jnp.zeros_like(dqt)

    own_k = jnp.zeros((tokens, HD), jnp.float32)
    own_v = jnp.zeros((tokens, HD), jnp.float32)
    for h in range(GROUP):
        part = pl.ds(h * tokens, tokens)
        own_k = own_k + cols[0, part, :] * q_ref[:, h * HD : (h + 1) * HD].astype(jnp.float32)
        own_v = own_v + cols[1, part, :] * do_ref[:, h * HD : (h + 1) * HD].astype(jnp.float32)
    ownk_ref[...] = own_k
    ownv_ref[...] = own_v
    qa[:, 0:HD] = qs16

    @pl.when(g == 0)
    def _():
        pl.semaphore_wait(barrier, chip + 1)

    def grad_step(c, _):
        key_t = kt[c]
        acc_k = jnp.zeros((CHUNK, HD), jnp.float32)
        acc_v = jnp.zeros((CHUNK, HD), jnp.float32)
        for r in range(0, rows, ROW_TILE):
            cut = slice(r, r + ROW_TILE)
            back = jnp.exp2(mc[c, :, cut] - st[2:3, cut])
            e = e_s[c, :, cut] * back
            ds = e * (gp_s[c, :, cut] - st[5:6, cut])
            e16 = e.astype(jnp.bfloat16)
            ds16 = ds.astype(jnp.bfloat16)
            acc_v = acc_v + dot_nn(e16, dor[cut, :])
            acc_k = acc_k + dot_nn(ds16, qa[cut, 0:HD])
            dqt[:, cut] = dqt[:, cut] + dot_nn(key_t, ds16)
        for b in range(CHUNK_BLOCKS):
            part = slice(b * SLOT_DEV, (b + 1) * SLOT_DEV)
            terms[g, chunk_chips * c + b // 2, b % 2, :, 0:HD] = acc_k[part].astype(jnp.bfloat16)
            terms[g, chunk_chips * c + b // 2, b % 2, :, HD : 2 * HD] = acc_v[part].astype(jnp.bfloat16)

        def swap(j, _):
            pair_copy(g, j).start()
            return 0

        lax.fori_loop(chunk_chips * c, jnp.minimum(chunk_chips * (c + 1), chip + 1), swap, 0)
        pl.when(c > 0)(lambda: pass_on(g, c - 1))
        return 0

    lax.fori_loop(0, chunks, grad_step, 0)
    pass_on(g, chunks - 1)

    kf = k_ref[...].astype(jnp.float32)
    for h in range(GROUP):
        cut = slice(h * tokens, (h + 1) * tokens)
        part = pl.ds(h * tokens, tokens)
        qs[part, :] = cols[0, part, :] * kf
    for r in range(0, rows, ROW_TILE):
        cut = slice(r, r + ROW_TILE)
        qs[cut, :] = qs[cut, :] + (dqt[:, cut] * st[6:7, cut]).T
    for h in range(GROUP):
        part = pl.ds(h * tokens, tokens)
        dq_ref[:, h * HD : (h + 1) * HD] = qs[part, :].astype(jnp.bfloat16)

    @pl.when(g == heads - 1)
    def _():
        for n in range(heads):
            cut = slice(2 * n * HD, 2 * (n + 1) * HD)
            out_ref[:, cut] = pair_sum(n, chip)

            def take(k, _):
                send_copy(n, k, k).wait_recv()
                out_ref[:, cut] = out_ref[:, cut] + got[n, k].astype(jnp.float32)
                return 0

            lax.fori_loop(chip + 1, chips, take, 0)

            def end_send(j, _):
                send_copy(n, j, chip).wait_send()
                return 0

            lax.fori_loop(0, chip, end_send, 0)

            def end_pair(j, _):
                pair_copy(n, j).wait_send()
                return 0

            lax.fori_loop(0, chip + 1, end_pair, 0)


def attend(q, do, k, v, seg, slots):
    tokens = q.shape[0]
    total = slots.shape[0]
    heads = k.shape[1] // HD
    rows = GROUP * tokens
    chunks = total // CHUNK
    wide = GROUP * HD
    by_head = lambda g: (0, g)
    f32, b16 = jnp.float32, jnp.bfloat16
    dma = pltpu.SemaphoreType.DMA
    chips = total // (2 * SLOT_DEV)
    block = (heads, chips, SLOT_DEV, 2 * HD)
    return pl.pallas_call(
        attend_kernel,
        grid=(heads,),
        in_specs=[
            pl.BlockSpec((tokens, wide), by_head),
            pl.BlockSpec((tokens, wide), by_head),
            pl.BlockSpec((tokens, HD), by_head),
            pl.BlockSpec((tokens, HD), by_head),
            pl.BlockSpec((heads, tokens), lambda g: (0, 0)),
            pl.BlockSpec((total, 2 * HD), by_head),
        ],
        out_specs=[
            pl.BlockSpec((tokens, wide), by_head),
            pl.BlockSpec((tokens, HD), by_head),
            pl.BlockSpec((tokens, HD), by_head),
            pl.BlockSpec((SLOT_DEV, 2 * heads * HD), lambda g: (0, 0)),
        ],
        out_shape=[
            jax.ShapeDtypeStruct(q.shape, b16),
            jax.ShapeDtypeStruct(k.shape, f32),
            jax.ShapeDtypeStruct(k.shape, f32),
            jax.ShapeDtypeStruct((SLOT_DEV, 2 * heads * HD), f32),
        ],
        scratch_shapes=[
            pltpu.VMEM((rows, 2 * HD), b16),
            pltpu.VMEM((rows, HD), b16),
            pltpu.VMEM((CHUNK, 2 * HD), b16),
            pltpu.VMEM((chunks, HD, CHUNK), b16),
            pltpu.VMEM((chunks, CHUNK, rows), f32),
            pltpu.VMEM((chunks, CHUNK, rows), f32),
            pltpu.VMEM((chunks, 1, rows), f32),
            pltpu.VMEM((8, rows), f32),
            pltpu.VMEM((HD, rows), f32),
            pltpu.VMEM((rows, HD), f32),
            pltpu.VMEM((rows, HD), f32),
            pltpu.VMEM((2, rows, HD), f32),
            pltpu.VMEM((heads, chips, 2, SLOT_DEV, 2 * HD), b16),
            pltpu.VMEM(block, b16),
            pltpu.VMEM(block, b16),
            pltpu.VMEM(block, b16),
            dma((heads, chips)),
            dma((heads, chips)),
            dma((heads, chips)),
            dma((heads, chips)),
        ],
        compiler_params=pltpu.CompilerParams(
            vmem_limit_bytes=63 * 1024 * 1024, collective_id=0, has_side_effects=True
        ),
        name="attend",
    )(q, do, k, v, seg, slots)


def enter_kernel(
    q_ref, do_ref, k_ref, v_ref, seg_ref,
    qo_ref, doo_ref, ko_ref, vo_ref, slots_ref,
    kb, vb, mine, stage, local_sem, x_send, x_recv, far_send, far_recv, ag_send, ag_recv, pair_send, pair_recv,
):
    heads = lax.axis_size("head")
    chips = lax.axis_size("ctx") // 2
    chunk_chips = CHUNK_BLOCKS // 2
    part = q_ref.shape[0]
    head = lax.axis_index("head")
    me = lax.axis_index("ctx")
    chip = me // 2
    core = me % 2
    low = chunk_chips * (chip // chunk_chips)
    high = low + chunk_chips
    partner = {"ctx": 2 * chip + 1 - core}
    peer = lambda k: {"ctx": 2 * k + core}

    def others(first, last, body):
        def step(k, _):
            pl.when(k != chip)(lambda: body(k))
            return 0

        lax.fori_loop(first, last, step, 0)

    barrier = pltpu.get_barrier_semaphore()
    greet = lambda device: pl.semaphore_signal(barrier, inc=1, device_id=device, device_id_type=MESH)
    for d in range(1, heads):
        greet({"head": (head + d) % heads})
    greet(partner)
    others(0, high, lambda k: greet(peer(k)))
    pl.semaphore_wait(barrier, heads + chips - low - 1)

    pairs = ((k_ref, kb), (v_ref, vb), (q_ref, qo_ref), (do_ref, doo_ref))

    def span(n, target):
        source, landing = pairs[n]
        wide = source.shape[1] // heads
        columns = pl.ds(pl.multiple_of(target * wide, HD), wide)
        rows = pl.ds(pl.multiple_of(head * part, 16), part)
        return source.at[:, columns], landing.at[rows, :]

    def cross(n, d):
        target = (head + d) % heads
        source, landing = span(n, target)
        return pltpu.make_async_remote_copy(
            src_ref=source,
            dst_ref=landing,
            send_sem=x_send.at[d, n],
            recv_sem=x_recv.at[d, n],
            device_id={"head": target},
            device_id_type=MESH,
        )

    def keep(n):
        return pltpu.make_async_copy(*span(n, head), local_sem.at[n])

    def far_out(n):
        way = 1 if n == 2 else heads - 1
        return pltpu.make_async_remote_copy(
            src_ref=span(n, (head + 2) % heads)[0],
            dst_ref=stage.at[n - 2],
            send_sem=far_send.at[n - 2],
            recv_sem=far_recv.at[n - 2],
            device_id={"head": (head + way) % heads},
            device_id_type=MESH,
        )

    def far_on(n):
        way = 1 if n == 2 else heads - 1
        rows = pl.ds(pl.multiple_of((head + heads - way) % heads * part, 16), part)
        return pltpu.make_async_remote_copy(
            src_ref=stage.at[n - 2],
            dst_ref=pairs[n][1].at[rows, :],
            send_sem=x_send.at[2, n],
            recv_sem=x_recv.at[2, n],
            device_id={"head": (head + way) % heads},
            device_id_type=MESH,
        )

    for n in range(2):
        for d in range(1, heads):
            cross(n, d).start()
        keep(n).start()
    for n in range(2):
        for d in range(1, heads):
            cross(n, d).wait_recv()
        keep(n).wait()
    for n in range(2, 4):
        far_out(n).start()
    for n in range(2, 4):
        for d in (1, 3):
            cross(n, d).start()
        keep(n).start()

    tokens = kb.shape[0]
    ko_ref[...] = kb[...]
    vo_ref[...] = vb[...]
    slot = lax.broadcasted_iota(jnp.int32, (SLOT_DEV, tokens), 0)
    for g in range(kb.shape[1] // HD):
        picks = (slot == seg_ref[g : g + 1, :]).astype(jnp.float32)
        counts = jnp.sum(picks, axis=1, keepdims=True)
        sizes = jnp.maximum(counts, 1.0)
        onehot = picks.astype(jnp.bfloat16)
        cut = slice(g * HD, (g + 1) * HD)
        keys = jnp.where(counts > 0, dot_nn(onehot, kb[:, cut]) / sizes, DEAD_KEY)
        values = dot_nn(onehot, vb[:, cut]) / sizes
        mine[:, 2 * g * HD : (2 * g + 1) * HD] = keys.astype(jnp.bfloat16)
        mine[:, (2 * g + 1) * HD : (2 * g + 2) * HD] = values.astype(jnp.bfloat16)

    def spread_copy(target, source):
        return pltpu.make_async_remote_copy(
            src_ref=mine,
            dst_ref=slots_ref.at[2 * source + core],
            send_sem=ag_send.at[target],
            recv_sem=ag_recv.at[source],
            device_id=peer(target),
            device_id_type=MESH,
        )

    def pair_copy(k, source):
        return pltpu.make_async_remote_copy(
            src_ref=source,
            dst_ref=slots_ref.at[2 * k + core],
            send_sem=pair_send.at[k],
            recv_sem=pair_recv.at[k],
            device_id=partner,
            device_id_type=MESH,
        )

    relay = lambda k: pair_copy(k, slots_ref.at[2 * k + core])
    arrive = lambda k: pltpu.make_async_remote_copy(
        src_ref=mine,
        dst_ref=slots_ref.at[2 * k + 1 - core],
        send_sem=pair_send.at[k],
        recv_sem=pair_recv.at[k],
        device_id=partner,
        device_id_type=MESH,
    )
    place = pltpu.make_async_copy(mine, slots_ref.at[me], local_sem.at[4])

    def start_spread(n, _):
        target = chips - 1 - n
        pl.when(target != chip)(lambda: spread_copy(target, chip).start())
        return 0

    lax.fori_loop(0, chips - low, start_spread, 0)
    for n in range(2, 4):
        far_out(n).wait_recv()
        far_on(n).start()
    pair_copy(chip, mine).start()
    place.start()

    def pass_on(k):
        spread_copy(k, k).wait_recv()
        relay(k).start()

    others(0, high, pass_on)
    place.wait()

    def end_pair(k, _):
        arrive(k).wait_recv()
        relay(k).wait_send()
        return 0

    lax.fori_loop(0, high, end_pair, 0)
    others(low, chips, lambda k: spread_copy(k, chip).wait_send())
    for n in range(2, 4):
        for d in range(1, heads):
            cross(n, d).wait_recv()
        keep(n).wait()
        far_out(n).wait_send()
        far_on(n).wait_send()
    for n in range(4):
        for d in range(1, heads):
            if n < 2 or d != 2:
                cross(n, d).wait_send()


def enter(q, do, k, v, seg):
    part, wide = q.shape
    narrow = k.shape[1]
    heads = lax.axis_size("head")
    shards = lax.axis_size("ctx")
    chips = shards // 2
    tokens = part * heads
    b16 = jnp.bfloat16
    vmem = pl.BlockSpec(memory_space=pltpu.VMEM)
    anywhere = pl.BlockSpec(memory_space=pl.ANY)
    dma = pltpu.SemaphoreType.DMA
    return pl.pallas_call(
        enter_kernel,
        in_specs=[vmem] * 5,
        out_specs=[anywhere, anywhere, vmem, vmem, anywhere],
        out_shape=[
            jax.ShapeDtypeStruct((tokens, wide // heads), b16),
            jax.ShapeDtypeStruct((tokens, wide // heads), b16),
            jax.ShapeDtypeStruct((tokens, narrow // heads), b16),
            jax.ShapeDtypeStruct((tokens, narrow // heads), b16),
            jax.ShapeDtypeStruct((shards, SLOT_DEV, 2 * narrow // heads), b16),
        ],
        scratch_shapes=[
            pltpu.VMEM((tokens, narrow // heads), b16),
            pltpu.VMEM((tokens, narrow // heads), b16),
            pltpu.VMEM((SLOT_DEV, 2 * narrow // heads), b16),
            pltpu.VMEM((2, part, wide // heads), b16),
            dma((5,)),
            dma((heads, 4)),
            dma((heads, 4)),
            dma((2,)),
            dma((2,)),
            dma((chips,)),
            dma((chips,)),
            dma((chips,)),
            dma((chips,)),
        ],
        compiler_params=pltpu.CompilerParams(collective_id=1, has_side_effects=True),
        name="enter",
    )(q, do, k, v, seg)


def local(queries, keys, values, segment_ids, grad_out):
    queries, grad_out, keys, values, slots = enter(queries, grad_out, keys, values, segment_ids)
    tokens = queries.shape[0]
    kv_heads = keys.shape[1] // HD
    slot_picks = segment_ids[:, :, None] == jnp.arange(SLOT_DEV, dtype=jnp.int32)[None, None, :]
    counts = jnp.sum(slot_picks.astype(jnp.int32), axis=1)
    grad_queries, own_k, own_v, slot_total = attend(
        queries, grad_out, keys, values, segment_ids, slots.reshape(-1, slots.shape[2])
    )
    slot_total = slot_total.reshape(SLOT_DEV, kv_heads, 2, HD)
    slot_spread = jnp.einsum(
        "gts,sgcd->tgcd",
        slot_picks.astype(jnp.float32),
        slot_total,
        precision=lax.Precision.HIGHEST,
    )
    token_sizes = jnp.sum(jnp.where(slot_picks, counts[:, None, :], 0), axis=2).T.astype(jnp.float32)
    spread = lambda n, own: (
        slot_spread[:, :, n] / token_sizes[..., None] + own.reshape(tokens, kv_heads, HD)
    ).astype(jnp.bfloat16).reshape(tokens, kv_heads * HD)
    return grad_queries, spread(0, own_k), spread(1, own_v)


def solution(mesh):
    both = P(("ctx", "head"), None)
    return jax.shard_map(
        local,
        mesh=mesh,
        in_specs=(both, both, both, P("head", "ctx"), both),
        out_specs=(P("ctx", "head"), P("ctx", "head"), P("ctx", "head")),
        check_vma=False,
    )
```
